512 devices in a mesh: seq: 64 (over z, y), dp: 8 (over x, core).
Axes of the slice: x: 4, y: 4, z: 16, core: 2. Of those that a mesh axis runs over, the one named last changes fastest.
Arguments:
- queries: bfloat16 [8, 8192, 2048], P('dp', 'seq'), may hold values from -40 to 40
- keys: bfloat16 [8, 8192, 2048], P('dp', 'seq'), may hold values from -6 to 6
- values: bfloat16 [8, 8192, 2048], P('dp', 'seq'), may hold values from -6 to 6
- grad_out: bfloat16 [8, 8192, 2048], P('dp', 'seq'), may hold values from -48 to 48
- lengths: int32 [8], P('dp'), may hold values from 1024 to 8192, as said below
- fields: int32 [8, 8192], P('dp', 'seq'), may hold values from 0 to 63
- field_bias: bfloat16 [16, 64], replicated, may hold values from -6 to 6
Outputs:
- grad_queries: bfloat16 [8, 8192, 2048], P('dp', 'seq')
- grad_keys: bfloat16 [8, 8192, 2048], P('dp', 'seq')
- grad_values: bfloat16 [8, 8192, 2048], P('dp', 'seq')
- grad_bias: float32 [16, 64], replicated
The draws below stay inside these ranges and needn't reach their ends.
Inputs may be any that keep to these rules, and one draw needn't show every extreme that they name: `lengths`: the valid positions of a sequence form a prefix; in every draw some sequence is full.
All inputs are finite; a program needn't handle non-finite values.
Results may differ from the reference program's by a relative error of at most 0.0077.
Values may be sent and summed in bfloat16 or wider, within the bound.
A program may use at most 128 MiB of HBM per device.

```python
import jax
import jax.numpy as jnp
from jax import lax

HEADS = 16
HEAD_DIM = 128
WINDOW = 512
FIELDS = 64
TOK_DEV = 128
SEQ_LEN = 8192
SEQS = 8


def key_field(key):
    inner_key = jax.random.fold_in(key, 11)
    full_shape = (SEQS, SEQ_LEN, HEADS * HEAD_DIM)
    drawn = jnp.clip(jax.random.normal(inner_key, full_shape, jnp.float32), -6.0, 6.0)
    return drawn


def draw_keys(key, part):
    return key_field(key).astype(jnp.bfloat16)


def draw_queries(key, part):
    inner_key = jax.random.fold_in(key, 12)
    full_shape = (SEQS, SEQ_LEN, HEADS * HEAD_DIM)
    drawn = jnp.clip(jax.random.normal(inner_key, full_shape, jnp.float32), -6.0, 6.0)
    return drawn.astype(jnp.bfloat16)


def draw_lengths(key, part):
    drawn = jax.random.randint(jax.random.fold_in(key, 21), (SEQS,), SEQ_LEN // 8, SEQ_LEN + 1, dtype=jnp.int32)
    chosen = jax.random.randint(jax.random.fold_in(key, 22), (), 0, SEQS, dtype=jnp.int32)
    places = jnp.arange(SEQS, dtype=jnp.int32)
    shortest = jnp.where(places == (chosen + 1) % SEQS, SEQ_LEN // 8, drawn)
    return jnp.where(places == chosen, SEQ_LEN, shortest).astype(jnp.int32)


def plant(entries, stream_key, least, high):
    place = [jax.random.randint(jax.random.fold_in(stream_key, axis), (), 0, length) for axis, length in enumerate(entries.shape)]
    longest = entries.shape.index(max(entries.shape))
    beside = place[:longest] + [(place[longest] + 1) % entries.shape[longest]] + place[longest + 1:]
    return entries.at[tuple(place)].set(least).at[tuple(beside)].set(high)


def levels(own_key, extent, cuts, smallest, high):
    def one(axis_at, parts):
        heights = jax.random.uniform(jax.random.fold_in(jax.random.fold_in(own_key, 6), axis_at), (parts,), jnp.float32, smallest / len(cuts), high / len(cuts))
        return jnp.repeat(jnp.exp(heights), extent[axis_at] // parts).reshape((-1,) + (1,) * (len(extent) - axis_at - 1))

    level = one(*cuts[0])
    for cut in cuts[1:]:
        level = level * one(*cut)
    return level


def scatter_about(rng, shape, scale, most, pieces=(), held_as=jnp.bfloat16):
    entries = jax.random.normal(rng, shape, jnp.float32) * scale
    if len(pieces) > 0:
        entries = levels(rng, shape, pieces, -0.22, 0.18) * entries
    return jnp.clip(entries, min=-most, max=most).astype(held_as)


def setup_inputs(seed: int = 0) -> dict:
    key_list = jax.random.split(jax.random.key(seed), 8)
    return {
        "queries": draw_queries(jax.random.fold_in(key_list[7], 71), 0),
        "keys": draw_keys(jax.random.fold_in(key_list[7], 71), 0),
        "values": scatter_about(key_list[2], (SEQS, SEQ_LEN, HEADS * HEAD_DIM), 1.0, 6.0, ((0, 8), (1, 64))),
        "grad_out": scatter_about(key_list[3], (SEQS, SEQ_LEN, HEADS * HEAD_DIM), 8.0, 48.0, ((0, 8), (1, 64))),
        "lengths": draw_lengths(jax.random.fold_in(key_list[7], 71), 0),
        "fields": plant(jax.random.randint(key_list[5], (SEQS, SEQ_LEN), 0, FIELDS), jax.random.fold_in(key_list[5], 1), 0, FIELDS - 1).astype(jnp.int32),
        "field_bias": scatter_about(key_list[6], (HEADS, FIELDS), 1.0, 6.0),
    }


def head_split(rows):
    return rows.reshape(rows.shape[0], HEADS, HEAD_DIM).astype(jnp.float32)


def band_mask(query_places, key_places, length):
    not_after = key_places[None, :] <= query_places[:, None]
    inside = key_places[None, :] > query_places[:, None] - WINDOW
    started = key_places[None, :] >= 0
    live_rows = query_places[:, None] < length
    return not_after & inside & started & live_rows


def block_grads(query_rows, key_rows, value_rows, grad_rows, key_bias, query_places, key_places, length):
    factor = HEAD_DIM ** -0.5
    query_heads = head_split(query_rows)
    key_heads = head_split(key_rows)
    value_heads = head_split(value_rows)
    grad_heads = head_split(grad_rows)
    logits = jnp.einsum("qhd,khd->hqk", query_heads, key_heads) * factor + key_bias[:, None, :]
    visible = band_mask(query_places, key_places, length)[None]
    row_peak = jnp.max(jnp.where(visible, logits, -1e30), axis=2, keepdims=True)
    powers = jnp.where(visible, jnp.exp(logits - row_peak), 0.0)
    live_rows = (query_places < length)[None, :, None]
    totals = jnp.where(live_rows, jnp.sum(powers, axis=2, keepdims=True), 1.0)
    attn_weights = powers / totals
    weights_low = lax.optimization_barrier(attn_weights.astype(jnp.bfloat16)).astype(jnp.float32)
    outputs = jnp.einsum("hqk,khd->qhd", weights_low, value_heads)
    row_delta = jnp.einsum("qhd,qhd->hq", grad_heads, outputs)
    grad_probs = jnp.einsum("qhd,khd->hqk", grad_heads, value_heads)
    grad_logits = attn_weights * (grad_probs - row_delta[:, :, None])
    grad_low = lax.optimization_barrier(grad_logits.astype(jnp.bfloat16)).astype(jnp.float32)
    grad_query = jnp.einsum("hqk,khd->qhd", grad_low, key_heads) * factor
    grad_key = jnp.einsum("hqk,qhd->khd", grad_low, query_heads) * factor
    grad_value = jnp.einsum("hqk,qhd->khd", weights_low, grad_heads)
    column = jnp.sum(grad_logits, axis=1)
    return grad_query, grad_key, grad_value, column


def reference(queries, keys, values, grad_out, lengths, fields, field_bias):
    bias_table = field_bias.astype(jnp.float32)
    row_width = HEADS * HEAD_DIM
    key_span = WINDOW + TOK_DEV

    def one_sequence(sequence_items):
        query_seq, key_seq, value_seq, grad_seq, length, field_seq = sequence_items
        key_pad = jnp.concatenate([jnp.zeros((WINDOW, row_width), key_seq.dtype), key_seq], axis=0)
        value_pad = jnp.concatenate([jnp.zeros((WINDOW, row_width), value_seq.dtype), value_seq], axis=0)
        field_pad = jnp.concatenate([jnp.full((WINDOW,), -1, jnp.int32), field_seq.astype(jnp.int32)], axis=0)

        def step(carry_state, block_number):
            key_acc, value_acc, bias_acc = carry_state
            first_row = (block_number * TOK_DEV).astype(jnp.int32)
            query_rows = lax.dynamic_slice_in_dim(query_seq, first_row, TOK_DEV, 0)
            grad_rows = lax.dynamic_slice_in_dim(grad_seq, first_row, TOK_DEV, 0)
            key_rows = lax.dynamic_slice_in_dim(key_pad, first_row, key_span, 0)
            value_rows = lax.dynamic_slice_in_dim(value_pad, first_row, key_span, 0)
            field_rows = lax.dynamic_slice_in_dim(field_pad, first_row, key_span, 0)
            onehot = (field_rows[:, None] == jnp.arange(FIELDS, dtype=jnp.int32)[None, :]).astype(jnp.float32)
            key_bias = jnp.dot(bias_table, onehot.T, precision=lax.Precision.HIGHEST)
            query_places = first_row + jnp.arange(TOK_DEV, dtype=jnp.int32)
            key_places = first_row - WINDOW + jnp.arange(key_span, dtype=jnp.int32)
            grad_query, grad_key, grad_value, column = block_grads(
                query_rows, key_rows, value_rows, grad_rows, key_bias, query_places, key_places, length)
            old_keys = lax.dynamic_slice_in_dim(key_acc, first_row, key_span, 0)
            key_acc = lax.dynamic_update_slice_in_dim(key_acc, old_keys + grad_key.reshape(key_span, row_width), first_row, 0)
            old_values = lax.dynamic_slice_in_dim(value_acc, first_row, key_span, 0)
            value_acc = lax.dynamic_update_slice_in_dim(value_acc, old_values + grad_value.reshape(key_span, row_width), first_row, 0)
            bias_acc = bias_acc + jnp.dot(column, onehot, precision=lax.Precision.HIGHEST)
            return (key_acc, value_acc, bias_acc), grad_query.reshape(TOK_DEV, row_width).astype(jnp.bfloat16)

        initial = (jnp.zeros((SEQ_LEN + WINDOW, row_width), jnp.float32),
                   jnp.zeros((SEQ_LEN + WINDOW, row_width), jnp.float32),
                   jnp.zeros((HEADS, FIELDS), jnp.float32))
        final_state, query_blocks = lax.scan(step, initial, jnp.arange(SEQ_LEN // TOK_DEV, dtype=jnp.int32))
        key_acc, value_acc, bias_acc = final_state
        return (query_blocks.reshape(SEQ_LEN, row_width), key_acc[WINDOW:].astype(jnp.bfloat16),
                value_acc[WINDOW:].astype(jnp.bfloat16), bias_acc)

    grad_queries, grad_keys, grad_values, bias_parts = lax.map(
        one_sequence, (queries, keys, values, grad_out, lengths, fields))
    return grad_queries, grad_keys, grad_values, jnp.sum(bias_parts, axis=0)
```

```python
import functools

import jax
import jax.numpy as jnp
from jax import lax
from jax.experimental import pallas as pl
from jax.experimental.pallas import tpu as pltpu
from jax.sharding import PartitionSpec as P

HEADS = 16
HEAD_DIM = 128
WINDOW = 512
FIELDS = 64
TOK = 128
GROUP = WINDOW // TOK
LOCAL_HEADS = HEADS // GROUP
SCALE = HEAD_DIM**-0.5
LOG2E = 1.4426950408889634
MASKED = -1e30
NT = (((1,), (1,)), ((), ()))
NN = (((1,), (0,)), ((), ()))
TN = (((0,), (0,)), ((), ()))


def dot(lhs, rhs, dims):
    return lax.dot_general(lhs, rhs, dims, preferred_element_type=jnp.float32)


def kernel(
    planes,
    copies,
    length_ref,
    bias_ref,
    fields_ref,
    q_hbm,
    k_hbm,
    v_hbm,
    g_hbm,
    dq_hbm,
    dk_hbm,
    dv_hbm,
    dbias_ref,
    bias_rows,
    bias_part,
    plane_parts,
    all_parts,
    kv,
    qg,
    field_rows,
    onehot,
    key_acc,
    own_acc,
    col_acc,
    ret_src,
    ret_dst,
    out_buf,
    field_send,
    field_recv,
    field_relay,
    field_halo,
    kv_send,
    kv_recv,
    qg_send,
    qg_recv,
    halo_send,
    halo_recv,
    ret_send,
    ret_recv,
    outq_send,
    outkv_send,
    out_recv,
    plane_send,
    plane_recv,
    all_send,
    all_recv,
):
    block = lax.axis_index("seq")
    sequence = lax.axis_index("dp")
    y = lax.rem(block, GROUP)
    z = block // GROUP
    has_prev = z > 0
    has_next = z < planes - 1

    def peer(step):
        other = lax.rem(y + step, GROUP)
        return other, {"seq": z * GROUP + other}

    nxt = {"seq": block + GROUP}
    prv = {"seq": block - GROUP}

    mates = copies * GROUP
    seat = sequence * GROUP + y

    def mate(step):
        other = lax.rem(seat + step, mates)
        return {"seq": z * GROUP + lax.rem(other, GROUP), "dp": other // GROUP}

    def above(step):
        return {"seq": lax.rem(z + step, planes) * GROUP + y}

    barrier = pltpu.get_barrier_semaphore()

    @pl.loop(1, mates)
    def _(step):
        pl.semaphore_signal(barrier, inc=1, device_id=mate(step))

    @pl.loop(1, planes)
    def _(step):
        pl.semaphore_signal(barrier, inc=1, device_id=above(step))

    pl.semaphore_wait(barrier, mates + planes - 2)

    own_rows = pl.ds(pl.multiple_of(y * TOK, TOK), TOK)
    own_keys = pl.ds(pl.multiple_of(WINDOW + y * TOK, TOK), TOK)
    plane_keys = pl.ds(WINDOW, WINDOW)

    def columns(owner, head):
        return pl.ds(pl.multiple_of((owner * LOCAL_HEADS + head) * HEAD_DIM, HEAD_DIM), HEAD_DIM)

    for step in range(1, GROUP):
        pltpu.make_async_remote_copy(
            fields_ref, field_rows.at[GROUP + y], field_send, field_recv, device_id=peer(step)[1]
        ).start()
    pltpu.make_async_copy(fields_ref, field_rows.at[GROUP + y], field_recv).start()

    for head in range(LOCAL_HEADS):
        for send, recv, sources, target, rows in (
            (kv_send, kv_recv, (k_hbm, v_hbm), kv, own_keys),
            (qg_send, qg_recv, (q_hbm, g_hbm), qg, own_rows),
        ):
            for step in range(1, GROUP):
                other, device = peer(step)
                for index, source in enumerate(sources):
                    pltpu.make_async_remote_copy(
                        source.at[:, columns(other, head)],
                        target.at[head, index, rows],
                        send.at[head],
                        recv.at[head],
                        device_id=device,
                    ).start()
            for index, source in enumerate(sources):
                pltpu.make_async_copy(
                    source.at[:, columns(y, head)], target.at[head, index, rows], recv.at[head]
                ).start()

    @pl.when(jnp.logical_not(has_prev))
    def _():
        kv[:, :, 0:WINDOW, :] = jnp.zeros((LOCAL_HEADS, 2, WINDOW, HEAD_DIM), kv.dtype)
        field_rows[0:GROUP] = jnp.full((GROUP, 1, TOK), -1, jnp.int32)

    plane_fields = field_rows.at[pl.ds(GROUP, GROUP)]
    halo_fields = field_rows.at[pl.ds(0, GROUP)]
    pltpu.make_async_copy(plane_fields, plane_fields, field_recv).wait()

    @pl.when(has_next)
    def _():
        pltpu.make_async_remote_copy(
            plane_fields, halo_fields, field_relay, field_halo, device_id=nxt
        ).start()

    def relay(head):
        arrived = kv.at[head, :, plane_keys]
        pltpu.make_async_copy(arrived, arrived, kv_recv.at[head]).wait()

        @pl.when(has_next)
        def _():
            pltpu.make_async_remote_copy(
                arrived,
                kv.at[head, :, pl.ds(0, WINDOW)],
                halo_send.at[head],
                halo_recv.at[head],
                device_id=nxt,
            ).start()

    relay(0)

    @pl.when(has_prev)
    def _():
        pltpu.make_async_copy(halo_fields, halo_fields, field_halo).wait()

    lane = lax.broadcasted_iota(jnp.int32, (TOK, TOK), 1)
    row = lax.broadcasted_iota(jnp.int32, (TOK, TOK), 0)
    for part in range(2 * GROUP):
        by_lane = jnp.broadcast_to(field_rows[part].astype(jnp.float32), (TOK, TOK))
        by_row = by_lane.T
        chosen = by_row == lax.rem(lane, FIELDS).astype(jnp.float32)
        onehot[part * TOK : (part + 1) * TOK] = chosen.astype(jnp.float32).astype(jnp.bfloat16)

    field = lax.broadcasted_iota(jnp.int32, (FIELDS, 2 * FIELDS), 0)
    place = lax.broadcasted_iota(jnp.int32, (FIELDS, 2 * FIELDS), 1)
    twice = (lax.rem(place, FIELDS) == field).astype(jnp.float32).astype(jnp.bfloat16)
    scaled = dot(bias_ref[...], twice, NN) / SCALE
    high_part = scaled.astype(jnp.bfloat16).astype(jnp.float32)
    is_high = lax.broadcasted_iota(jnp.int32, (HEADS, 2 * FIELDS), 1) < FIELDS
    bias_rows[...] = jnp.where(is_high, high_part, scaled - high_part)
    bias_part[...] = jnp.zeros_like(bias_part)

    older = row > lane
    length = length_ref[0]
    unseen = jnp.where(has_prev, 0.0, MASKED)

    def work(head):
        here = qg.at[head]
        pltpu.make_async_copy(here, here, qg_recv.at[head]).wait()

        @pl.when(has_prev)
        def _():
            halo = kv.at[head, :, pl.ds(0, WINDOW)]
            pltpu.make_async_copy(halo, halo, halo_recv.at[head]).wait()

        bias_row = bias_rows[pl.ds(y * LOCAL_HEADS + head, 1), :]
        bias_block = jnp.broadcast_to(bias_row, (TOK, TOK)).astype(jnp.bfloat16)
        for part in range(GROUP):
            first = part * TOK
            span = WINDOW + TOK
            seen = pl.ds(first, span)
            queries = qg[head, 0, first : first + TOK, :]
            grads = qg[head, 1, first : first + TOK, :]
            keys = kv[head, 0, seen, :]
            values = kv[head, 1, seen, :]
            logits = dot(
                jnp.concatenate([keys, onehot[seen, :]], axis=1),
                jnp.concatenate([queries, bias_block], axis=1),
                NT,
            )
            probs_grad = dot(values, grads, NT)

            def tiles(full):
                merged = jnp.where(older, full[0:TOK], full[WINDOW:span])
                return [merged] + [full[t * TOK : (t + 1) * TOK] for t in range(1, GROUP)]

            logit_tiles = tiles(logits)
            halo_tiles = GROUP - part
            logit_tiles = [
                (jnp.where(older, tile + unseen, tile) if t == 0 else tile + unseen)
                if t < halo_tiles
                else tile
                for t, tile in enumerate(logit_tiles)
            ]
            logit = jnp.concatenate(logit_tiles, axis=0)
            peak = jnp.max(logit, axis=0, keepdims=True)
            power = jnp.exp2((logit - peak) * (SCALE * LOG2E))
            total = jnp.sum(power, axis=0, keepdims=True)
            place = z * WINDOW + first + lax.broadcasted_iota(jnp.int32, (1, TOK), 1)
            share = jnp.where(place < length, 1.0 / total, 0.0)
            weight = power * share
            weight_low = weight.astype(jnp.bfloat16)
            prob = jnp.concatenate(tiles(probs_grad), axis=0)
            delta = jnp.sum(weight_low.astype(jnp.float32) * prob, axis=0, keepdims=True)
            grad = weight * (prob - delta)

            def spread(merged):
                top = merged[0:TOK]
                none = jnp.zeros_like(top)
                return jnp.concatenate(
                    [jnp.where(older, top, none), merged[TOK:WINDOW], jnp.where(older, none, top)],
                    axis=0,
                )

            grad_full = spread(grad)
            grad_low = grad_full.astype(jnp.bfloat16)
            weight_full = spread(weight_low.astype(jnp.float32)).astype(jnp.bfloat16)
            query_grad = dot(grad_low, keys, TN) * SCALE
            out_buf[head, 0, first : first + TOK, :] = query_grad.astype(jnp.bfloat16)
            key_part = dot(grad_low, queries, NN)
            value_part = dot(weight_full, grads, NN)
            for store, fresh in ((key_acc.at[0], key_part), (key_acc.at[1], value_part), (col_acc, grad_full)):
                if part == 0:
                    store[0:span, :] = fresh
                else:
                    store[first : first + WINDOW, :] += fresh[0:WINDOW]
                    store[first + WINDOW : first + span, :] = fresh[WINDOW:span]

        ret_src[head, 0] = (key_acc[0, 0:WINDOW] * SCALE).astype(jnp.bfloat16)
        ret_src[head, 1] = key_acc[1, 0:WINDOW].astype(jnp.bfloat16)

        @pl.when(has_prev)
        def _():
            pltpu.make_async_remote_copy(
                ret_src.at[head],
                ret_dst.at[head],
                ret_send.at[head],
                ret_recv.at[head],
                device_id=prv,
            ).start()

        own_acc[head, 0] = key_acc[0, WINDOW:] * SCALE
        own_acc[head, 1] = key_acc[1, WINDOW:]

        for step in range(1, GROUP):
            other, device = peer(step)
            pltpu.make_async_remote_copy(
                out_buf.at[head, 0, pl.ds(pl.multiple_of(other * TOK, TOK), TOK)],
                dq_hbm.at[:, columns(y, head)],
                outq_send.at[head],
                out_recv.at[0],
                device_id=device,
            ).start()
        pltpu.make_async_copy(
            out_buf.at[head, 0, own_rows], dq_hbm.at[:, columns(y, head)], out_recv.at[0]
        ).start()

        sums = col_acc[...]
        high = sums.astype(jnp.bfloat16)
        low = (sums - high.astype(jnp.float32)).astype(jnp.bfloat16)
        by_query = dot(high, onehot[...], TN) + dot(low, onehot[...], TN)
        bias_part[pl.ds(head, 1), :] = jnp.sum(by_query, axis=0, keepdims=True)

    def finish(head):
        @pl.when(has_next)
        def _():
            back = ret_dst.at[head]
            pltpu.make_async_copy(back, back, ret_recv.at[head]).wait()
            for index in range(2):
                out_buf[head, 1 + index] = (
                    own_acc[head, index] + ret_dst[head, index].astype(jnp.float32)
                ).astype(jnp.bfloat16)

        @pl.when(jnp.logical_not(has_next))
        def _():
            for index in range(2):
                out_buf[head, 1 + index] = own_acc[head, index].astype(jnp.bfloat16)

        for index, result in ((1, dk_hbm), (2, dv_hbm)):
            for step in range(1, GROUP):
                other, device = peer(step)
                pltpu.make_async_remote_copy(
                    out_buf.at[head, index, pl.ds(pl.multiple_of(other * TOK, TOK), TOK)],
                    result.at[:, columns(y, head)],
                    outkv_send.at[head],
                    out_recv.at[index],
                    device_id=device,
                ).start()
            pltpu.make_async_copy(
                out_buf.at[head, index, own_rows], result.at[:, columns(y, head)], out_recv.at[index]
            ).start()

    @pl.loop(0, LOCAL_HEADS)
    def _(head):
        @pl.when(head + 1 < LOCAL_HEADS)
        def _():
            relay(head + 1)

        work(head)

        @pl.when(head == LOCAL_HEADS - 1)
        def _():
            plane_parts[seat] = bias_part[...]

            @pl.loop(1, mates)
            def _(step):
                pltpu.make_async_remote_copy(
                    bias_part, plane_parts.at[seat], plane_send, plane_recv, device_id=mate(step)
                ).start()

        @pl.when(head > 0)
        def _():
            finish(head - 1)

    others = plane_parts.at[pl.ds(0, mates - 1)]
    pltpu.make_async_copy(others, others, plane_recv).wait()
    for owner in range(GROUP):
        total = plane_parts[owner]
        for copy in range(1, copies):
            total = total + plane_parts[copy * GROUP + owner]
        first = owner * LOCAL_HEADS
        all_parts[z, first : first + LOCAL_HEADS, :] = total[0:LOCAL_HEADS]

    @pl.loop(1, planes)
    def _(step):
        mine = all_parts.at[z]
        pltpu.make_async_remote_copy(mine, mine, all_send, all_recv, device_id=above(step)).start()

    finish(LOCAL_HEADS - 1)

    rest = all_parts.at[pl.ds(0, planes - 1)]
    pltpu.make_async_copy(rest, rest, all_recv).wait()
    bias_total = all_parts[0]
    for plane in range(1, planes):
        bias_total = bias_total + all_parts[plane]
    dbias_ref[...] = bias_total[:, 0:FIELDS]

    pltpu.make_async_copy(others, others, plane_send).wait()
    pltpu.make_async_copy(rest, rest, all_send).wait()
    sent_fields = field_rows.at[pl.ds(0, GROUP - 1)]
    pltpu.make_async_copy(sent_fields, sent_fields, field_send).wait()

    @pl.when(has_next)
    def _():
        pltpu.make_async_copy(halo_fields, halo_fields, field_relay).wait()

    @pl.loop(0, LOCAL_HEADS)
    def _(head):
        sent = kv.at[head, :, pl.ds(0, WINDOW - TOK)]
        pltpu.make_async_copy(sent, sent, kv_send.at[head]).wait()
        pltpu.make_async_copy(sent, sent, qg_send.at[head]).wait()
        pltpu.make_async_copy(sent, sent, outkv_send.at[head]).wait()
        query_sent = kv.at[head, 0, pl.ds(0, WINDOW - TOK)]
        pltpu.make_async_copy(query_sent, query_sent, outq_send.at[head]).wait()

        @pl.when(has_next)
        def _():
            halo = kv.at[head, :, pl.ds(0, WINDOW)]
            pltpu.make_async_copy(halo, halo, halo_send.at[head]).wait()

        @pl.when(has_prev)
        def _():
            source = ret_src.at[head]
            pltpu.make_async_copy(source, source, ret_send.at[head]).wait()

    for index, result in enumerate((dq_hbm, dk_hbm, dv_hbm)):
        pltpu.make_async_copy(result, result, out_recv.at[index]).wait()


def copy_kernel(*refs):
    count = len(refs) // 2
    sources, targets, sems = refs[:count], refs[count : 2 * count], refs[-1]
    moves = [
        pltpu.make_async_copy(sources[index], targets[index], sems.at[index]) for index in range(count)
    ]
    for move in moves:
        move.start()
    for move in moves:
        move.wait()


def shards(planes, copies, queries, keys, values, grad_out, lengths, fields, field_bias):
    tok_rows, row_width = queries.shape[1:]
    low_type, full_type = jnp.bfloat16, jnp.float32
    grads_shape = jax.ShapeDtypeStruct((tok_rows, row_width), low_type)
    anywhere = pl.BlockSpec(memory_space=pl.ANY)
    in_vmem = pl.BlockSpec(memory_space=pltpu.VMEM)
    dma = pltpu.SemaphoreType.DMA
    heads = LOCAL_HEADS
    query_grad, key_grad, value_grad, bias_total = pl.pallas_call(
        functools.partial(kernel, planes, copies),
        out_shape=(
            grads_shape,
            grads_shape,
            grads_shape,
            jax.ShapeDtypeStruct((HEADS, FIELDS), full_type),
        ),
        in_specs=[
            pl.BlockSpec(memory_space=pltpu.SMEM),
            in_vmem,
            in_vmem,
            anywhere,
            anywhere,
            anywhere,
            anywhere,
        ],
        out_specs=(anywhere, anywhere, anywhere, in_vmem),
        scratch_shapes=[
            pltpu.VMEM((HEADS, 2 * FIELDS), full_type),
            pltpu.VMEM((8, 2 * FIELDS), full_type),
            pltpu.VMEM((copies * GROUP, 8, 2 * FIELDS), full_type),
            pltpu.VMEM((planes, HEADS, 2 * FIELDS), full_type),
            pltpu.VMEM((heads, 2, 2 * WINDOW, HEAD_DIM), low_type),
            pltpu.VMEM((heads, 2, WINDOW, HEAD_DIM), low_type),
            pltpu.VMEM((2 * GROUP, 1, TOK), jnp.int32),
            pltpu.VMEM((2 * WINDOW, 2 * FIELDS), low_type),
            pltpu.VMEM((2, 2 * WINDOW, HEAD_DIM), full_type),
            pltpu.VMEM((heads, 2, WINDOW, HEAD_DIM), full_type),
            pltpu.VMEM((2 * WINDOW, HEAD_DIM), full_type),
            pltpu.VMEM((heads, 2, WINDOW, HEAD_DIM), low_type),
            pltpu.VMEM((heads, 2, WINDOW, HEAD_DIM), low_type),
            pltpu.VMEM((heads, 3, WINDOW, HEAD_DIM), low_type),
            dma,
            dma,
            dma,
            dma,
            dma((heads,)),
            dma((heads,)),
            dma((heads,)),
            dma((heads,)),
            dma((heads,)),
            dma((heads,)),
            dma((heads,)),
            dma((heads,)),
            dma((heads,)),
            dma((heads,)),
            dma((3,)),
            dma,
            dma,
            dma,
            dma,
        ],
        compiler_params=pltpu.CompilerParams(
            collective_id=0, has_side_effects=True, vmem_limit_bytes=56 * 2**20
        ),
    )(lengths, field_bias, fields, queries[0], keys[0], values[0], grad_out[0])
    results = (query_grad, key_grad, value_grad, bias_total)
    query_grad, key_grad, value_grad, bias_total = pl.pallas_call(
        copy_kernel,
        out_shape=tuple(jax.ShapeDtypeStruct(one.shape, one.dtype) for one in results),
        in_specs=[anywhere] * 4,
        out_specs=(anywhere,) * 4,
        scratch_shapes=[dma((4,))],
        compiler_params=pltpu.CompilerParams(vmem_limit_bytes=56 * 2**20),
    )(*results)
    return query_grad[None], key_grad[None], value_grad[None], bias_total


def solution(mesh):
    rows = P("dp", "seq", None)
    return jax.shard_map(
        functools.partial(shards, mesh.shape["seq"] // GROUP, mesh.shape["dp"]),
        mesh=mesh,
        in_specs=(rows, rows, rows, rows, P("dp"), P("dp", "seq"), P()),
        out_specs=(rows, rows, rows, P()),
        check_vma=False,
    )
```

```python
import functools

import jax
import jax.numpy as jnp
from jax import lax
from jax.experimental import pallas as pl
from jax.experimental.pallas import tpu as pltpu
from jax.sharding import PartitionSpec as P

HEADS = 16
HEAD_DIM = 128
WINDOW = 512
FIELDS = 64
TOK = 128
GROUP = WINDOW // TOK
LOCAL_HEADS = HEADS // GROUP
SCALE = HEAD_DIM**-0.5
LOG2E = 1.4426950408889634
MASKED = -1e30
NT = (((1,), (1,)), ((), ()))
NN = (((1,), (0,)), ((), ()))
TN = (((0,), (0,)), ((), ()))


def dot(lhs, rhs, dims):
    return lax.dot_general(lhs, rhs, dims, preferred_element_type=jnp.float32)


def kernel(
    planes,
    copies,
    length_ref,
    bias_ref,
    fields_ref,
    q_hbm,
    k_hbm,
    v_hbm,
    g_hbm,
    dq_ref,
    dk_ref,
    dv_ref,
    dbias_ref,
    bias_rows,
    bias_part,
    plane_parts,
    all_parts,
    kv,
    qg,
    field_rows,
    onehot,
    key_acc,
    own_acc,
    col_acc,
    ret_src,
    ret_dst,
    out_buf,
    field_send,
    field_recv,
    field_relay,
    field_halo,
    kv_send,
    kv_recv,
    qg_send,
    qg_recv,
    halo_send,
    halo_recv,
    ret_send,
    ret_recv,
    outq_send,
    outkv_send,
    out_recv,
    plane_send,
    plane_recv,
    all_send,
    all_recv,
):
    block = lax.axis_index("seq")
    sequence = lax.axis_index("dp")
    y = lax.rem(block, GROUP)
    z = block // GROUP
    has_prev = z > 0
    has_next = z < planes - 1

    def peer(step):
        other = lax.rem(y + step, GROUP)
        return other, {"seq": z * GROUP + other}

    nxt = {"seq": block + GROUP}
    prv = {"seq": block - GROUP}

    mates = copies * GROUP
    seat = sequence * GROUP + y

    def mate(step):
        other = lax.rem(seat + step, mates)
        return {"seq": z * GROUP + lax.rem(other, GROUP), "dp": other // GROUP}

    def above(step):
        return {"seq": lax.rem(z + step, planes) * GROUP + y}

    barrier = pltpu.get_barrier_semaphore()

    @pl.loop(1, mates)
    def _(step):
        pl.semaphore_signal(barrier, inc=1, device_id=mate(step))

    @pl.loop(1, planes)
    def _(step):
        pl.semaphore_signal(barrier, inc=1, device_id=above(step))

    pl.semaphore_wait(barrier, mates + planes - 2)

    own_rows = pl.ds(pl.multiple_of(y * TOK, TOK), TOK)
    own_keys = pl.ds(pl.multiple_of(WINDOW + y * TOK, TOK), TOK)
    plane_keys = pl.ds(WINDOW, WINDOW)

    def columns(owner, head):
        return pl.ds(pl.multiple_of((owner * LOCAL_HEADS + head) * HEAD_DIM, HEAD_DIM), HEAD_DIM)

    for step in range(1, GROUP):
        pltpu.make_async_remote_copy(
            fields_ref, field_rows.at[GROUP + y], field_send, field_recv, device_id=peer(step)[1]
        ).start()
    pltpu.make_async_copy(fields_ref, field_rows.at[GROUP + y], field_recv).start()

    for head in range(LOCAL_HEADS):
        for send, recv, sources, target, rows in (
            (kv_send, kv_recv, (k_hbm, v_hbm), kv, own_keys),
            (qg_send, qg_recv, (q_hbm, g_hbm), qg, own_rows),
        ):
            for step in range(1, GROUP):
                other, device = peer(step)
                for index, source in enumerate(sources):
                    pltpu.make_async_remote_copy(
                        source.at[:, columns(other, head)],
                        target.at[head, index, rows],
                        send.at[head],
                        recv.at[head],
                        device_id=device,
                    ).start()
            for index, source in enumerate(sources):
                pltpu.make_async_copy(
                    source.at[:, columns(y, head)], target.at[head, index, rows], recv.at[head]
                ).start()

    @pl.when(jnp.logical_not(has_prev))
    def _():
        kv[:, :, 0:WINDOW, :] = jnp.zeros((LOCAL_HEADS, 2, WINDOW, HEAD_DIM), kv.dtype)
        field_rows[0:GROUP] = jnp.full((GROUP, 1, TOK), -1, jnp.int32)

    plane_fields = field_rows.at[pl.ds(GROUP, GROUP)]
    halo_fields = field_rows.at[pl.ds(0, GROUP)]
    pltpu.make_async_copy(plane_fields, plane_fields, field_recv).wait()

    @pl.when(has_next)
    def _():
        pltpu.make_async_remote_copy(
            plane_fields, halo_fields, field_relay, field_halo, device_id=nxt
        ).start()

    def relay(head):
        arrived = kv.at[head, :, plane_keys]
        pltpu.make_async_copy(arrived, arrived, kv_recv.at[head]).wait()

        @pl.when(has_next)
        def _():
            pltpu.make_async_remote_copy(
                arrived,
                kv.at[head, :, pl.ds(0, WINDOW)],
                halo_send.at[head],
                halo_recv.at[head],
                device_id=nxt,
            ).start()

    relay(0)

    @pl.when(has_prev)
    def _():
        pltpu.make_async_copy(halo_fields, halo_fields, field_halo).wait()

    lane = lax.broadcasted_iota(jnp.int32, (TOK, TOK), 1)
    row = lax.broadcasted_iota(jnp.int32, (TOK, TOK), 0)
    for part in range(2 * GROUP):
        by_lane = jnp.broadcast_to(field_rows[part].astype(jnp.float32), (TOK, TOK))
        by_row = by_lane.T
        chosen = by_row == lax.rem(lane, FIELDS).astype(jnp.float32)
        onehot[part * TOK : (part + 1) * TOK] = chosen.astype(jnp.float32).astype(jnp.bfloat16)

    field = lax.broadcasted_iota(jnp.int32, (FIELDS, 2 * FIELDS), 0)
    place = lax.broadcasted_iota(jnp.int32, (FIELDS, 2 * FIELDS), 1)
    twice = (lax.rem(place, FIELDS) == field).astype(jnp.float32).astype(jnp.bfloat16)
    scaled = dot(bias_ref[...], twice, NN) / SCALE
    high_part = scaled.astype(jnp.bfloat16).astype(jnp.float32)
    is_high = lax.broadcasted_iota(jnp.int32, (HEADS, 2 * FIELDS), 1) < FIELDS
    bias_rows[...] = jnp.where(is_high, high_part, scaled - high_part)
    bias_part[...] = jnp.zeros_like(bias_part)

    older = row > lane
    length = length_ref[0]
    unseen = jnp.where(has_prev, 0.0, MASKED)

    def work(head):
        here = qg.at[head]
        pltpu.make_async_copy(here, here, qg_recv.at[head]).wait()

        @pl.when(has_prev)
        def _():
            halo = kv.at[head, :, pl.ds(0, WINDOW)]
            pltpu.make_async_copy(halo, halo, halo_recv.at[head]).wait()

        bias_row = bias_rows[pl.ds(y * LOCAL_HEADS + head, 1), :]
        bias_block = jnp.broadcast_to(bias_row, (TOK, TOK)).astype(jnp.bfloat16)
        for part in range(GROUP):
            first = part * TOK
            span = WINDOW + TOK
            seen = pl.ds(first, span)
            queries = qg[head, 0, first : first + TOK, :]
            grads = qg[head, 1, first : first + TOK, :]
            keys = kv[head, 0, seen, :]
            values = kv[head, 1, seen, :]
            logits = dot(
                jnp.concatenate([keys, onehot[seen, :]], axis=1),
                jnp.concatenate([queries, bias_block], axis=1),
                NT,
            )
            probs_grad = dot(values, grads, NT)

            def tiles(full):
                merged = jnp.where(older, full[0:TOK], full[WINDOW:span])
                return [merged] + [full[t * TOK : (t + 1) * TOK] for t in range(1, GROUP)]

            logit_tiles = tiles(logits)
            halo_tiles = GROUP - part
            logit_tiles = [
                (jnp.where(older, tile + unseen, tile) if t == 0 else tile + unseen)
                if t < halo_tiles
                else tile
                for t, tile in enumerate(logit_tiles)
            ]
            logit = jnp.concatenate(logit_tiles, axis=0)
            peak = jnp.max(logit, axis=0, keepdims=True)
            power = jnp.exp2((logit - peak) * (SCALE * LOG2E))
            total = jnp.sum(power, axis=0, keepdims=True)
            place = z * WINDOW + first + lax.broadcasted_iota(jnp.int32, (1, TOK), 1)
            share = jnp.where(place < length, 1.0 / total, 0.0)
            weight = power * share
            weight_low = weight.astype(jnp.bfloat16)
            prob = jnp.concatenate(tiles(probs_grad), axis=0)
            delta = jnp.sum(weight_low.astype(jnp.float32) * prob, axis=0, keepdims=True)
            grad = weight * (prob - delta)

            def spread(merged):
                top = merged[0:TOK]
                none = jnp.zeros_like(top)
                return jnp.concatenate(
                    [jnp.where(older, top, none), merged[TOK:WINDOW], jnp.where(older, none, top)],
                    axis=0,
                )

            grad_full = spread(grad)
            grad_low = grad_full.astype(jnp.bfloat16)
            weight_full = spread(weight_low.astype(jnp.float32)).astype(jnp.bfloat16)
            query_grad = dot(grad_low, keys, TN) * SCALE
            out_buf[head, 0, first : first + TOK, :] = query_grad.astype(jnp.bfloat16)
            key_part = dot(grad_low, queries, NN)
            value_part = dot(weight_full, grads, NN)
            for store, fresh in ((key_acc.at[0], key_part), (key_acc.at[1], value_part), (col_acc, grad_full)):
                if part == 0:
                    store[0:span, :] = fresh
                else:
                    store[first : first + WINDOW, :] += fresh[0:WINDOW]
                    store[first + WINDOW : first + span, :] = fresh[WINDOW:span]

        ret_src[head, 0] = (key_acc[0, 0:WINDOW] * SCALE).astype(jnp.bfloat16)
        ret_src[head, 1] = key_acc[1, 0:WINDOW].astype(jnp.bfloat16)

        @pl.when(has_prev)
        def _():
            pltpu.make_async_remote_copy(
                ret_src.at[head],
                ret_dst.at[head],
                ret_send.at[head],
                ret_recv.at[head],
                device_id=prv,
            ).start()

        own_acc[head, 0] = key_acc[0, WINDOW:] * SCALE
        own_acc[head, 1] = key_acc[1, WINDOW:]

        for step in range(1, GROUP):
            other, device = peer(step)
            pltpu.make_async_remote_copy(
                out_buf.at[head, 0, pl.ds(pl.multiple_of(other * TOK, TOK), TOK)],
                dq_ref.at[:, columns(y, head)],
                outq_send.at[head],
                out_recv.at[0],
                device_id=device,
            ).start()
        pltpu.make_async_copy(
            out_buf.at[head, 0, own_rows], dq_ref.at[:, columns(y, head)], out_recv.at[0]
        ).start()

        sums = col_acc[...]
        high = sums.astype(jnp.bfloat16)
        low = (sums - high.astype(jnp.float32)).astype(jnp.bfloat16)
        by_query = dot(high, onehot[...], TN) + dot(low, onehot[...], TN)
        bias_part[pl.ds(head, 1), :] = jnp.sum(by_query, axis=0, keepdims=True)

    def finish(head):
        @pl.when(has_next)
        def _():
            back = ret_dst.at[head]
            pltpu.make_async_copy(back, back, ret_recv.at[head]).wait()
            for index in range(2):
                out_buf[head, 1 + index] = (
                    own_acc[head, index] + ret_dst[head, index].astype(jnp.float32)
                ).astype(jnp.bfloat16)

        @pl.when(jnp.logical_not(has_next))
        def _():
            for index in range(2):
                out_buf[head, 1 + index] = own_acc[head, index].astype(jnp.bfloat16)

        for index, result in ((1, dk_ref), (2, dv_ref)):
            for step in range(1, GROUP):
                other, device = peer(step)
                pltpu.make_async_remote_copy(
                    out_buf.at[head, index, pl.ds(pl.multiple_of(other * TOK, TOK), TOK)],
                    result.at[:, columns(y, head)],
                    outkv_send.at[head],
                    out_recv.at[index],
                    device_id=device,
                ).start()
            pltpu.make_async_copy(
                out_buf.at[head, index, own_rows], result.at[:, columns(y, head)], out_recv.at[index]
            ).start()

    @pl.loop(0, LOCAL_HEADS)
    def _(head):
        @pl.when(head + 1 < LOCAL_HEADS)
        def _():
            relay(head + 1)

        work(head)

        @pl.when(head == LOCAL_HEADS - 1)
        def _():
            plane_parts[seat] = bias_part[...]

            @pl.loop(1, mates)
            def _(step):
                pltpu.make_async_remote_copy(
                    bias_part, plane_parts.at[seat], plane_send, plane_recv, device_id=mate(step)
                ).start()

        @pl.when(head > 0)
        def _():
            finish(head - 1)

    others = plane_parts.at[pl.ds(0, mates - 1)]
    pltpu.make_async_copy(others, others, plane_recv).wait()
    for owner in range(GROUP):
        total = plane_parts[owner]
        for copy in range(1, copies):
            total = total + plane_parts[copy * GROUP + owner]
        first = owner * LOCAL_HEADS
        all_parts[z, first : first + LOCAL_HEADS, :] = total[0:LOCAL_HEADS]

    @pl.loop(1, planes)
    def _(step):
        mine = all_parts.at[z]
        pltpu.make_async_remote_copy(mine, mine, all_send, all_recv, device_id=above(step)).start()

    finish(LOCAL_HEADS - 1)

    rest = all_parts.at[pl.ds(0, planes - 1)]
    pltpu.make_async_copy(rest, rest, all_recv).wait()
    bias_total = all_parts[0]
    for plane in range(1, planes):
        bias_total = bias_total + all_parts[plane]
    dbias_ref[...] = bias_total[:, 0:FIELDS]

    pltpu.make_async_copy(others, others, plane_send).wait()
    pltpu.make_async_copy(rest, rest, all_send).wait()
    sent_fields = field_rows.at[pl.ds(0, GROUP - 1)]
    pltpu.make_async_copy(sent_fields, sent_fields, field_send).wait()

    @pl.when(has_next)
    def _():
        pltpu.make_async_copy(halo_fields, halo_fields, field_relay).wait()

    @pl.loop(0, LOCAL_HEADS)
    def _(head):
        sent = kv.at[head, :, pl.ds(0, WINDOW - TOK)]
        pltpu.make_async_copy(sent, sent, kv_send.at[head]).wait()
        pltpu.make_async_copy(sent, sent, qg_send.at[head]).wait()
        pltpu.make_async_copy(sent, sent, outkv_send.at[head]).wait()
        query_sent = kv.at[head, 0, pl.ds(0, WINDOW - TOK)]
        pltpu.make_async_copy(query_sent, query_sent, outq_send.at[head]).wait()

        @pl.when(has_next)
        def _():
            halo = kv.at[head, :, pl.ds(0, WINDOW)]
            pltpu.make_async_copy(halo, halo, halo_send.at[head]).wait()

        @pl.when(has_prev)
        def _():
            source = ret_src.at[head]
            pltpu.make_async_copy(source, source, ret_send.at[head]).wait()

    for index, result in enumerate((dq_ref, dk_ref, dv_ref)):
        pltpu.make_async_copy(result, result, out_recv.at[index]).wait()


def copy_kernel(*refs):
    count = len(refs) // 2
    sources, targets, sems = refs[:count], refs[count : 2 * count], refs[-1]
    moves = [
        pltpu.make_async_copy(sources[index], targets[index], sems.at[index]) for index in range(count)
    ]
    for move in moves:
        move.start()
    for move in moves:
        move.wait()


def shards(planes, copies, queries, keys, values, grad_out, lengths, fields, field_bias):
    tok_rows, row_width = queries.shape[1:]
    low_type, full_type = jnp.bfloat16, jnp.float32
    grads_shape = jax.ShapeDtypeStruct((tok_rows, row_width), low_type)
    in_hbm = pl.BlockSpec(memory_space=pltpu.HBM)
    in_vmem = pl.BlockSpec(memory_space=pltpu.VMEM)
    dma = pltpu.SemaphoreType.DMA
    heads = LOCAL_HEADS
    query_grad, key_grad, value_grad, bias_total = pl.pallas_call(
        functools.partial(kernel, planes, copies),
        out_shape=(
            pltpu.VMEM(grads_shape.shape, low_type),
            pltpu.VMEM(grads_shape.shape, low_type),
            pltpu.VMEM(grads_shape.shape, low_type),
            pltpu.VMEM((HEADS, FIELDS), full_type),
        ),
        in_specs=[
            pl.BlockSpec(memory_space=pltpu.SMEM),
            in_vmem,
            in_vmem,
            in_hbm,
            in_hbm,
            in_hbm,
            in_hbm,
        ],
        out_specs=(in_vmem, in_vmem, in_vmem, in_vmem),
        scratch_shapes=[
            pltpu.VMEM((HEADS, 2 * FIELDS), full_type),
            pltpu.VMEM((8, 2 * FIELDS), full_type),
            pltpu.VMEM((copies * GROUP, 8, 2 * FIELDS), full_type),
            pltpu.VMEM((planes, HEADS, 2 * FIELDS), full_type),
            pltpu.VMEM((heads, 2, 2 * WINDOW, HEAD_DIM), low_type),
            pltpu.VMEM((heads, 2, WINDOW, HEAD_DIM), low_type),
            pltpu.VMEM((2 * GROUP, 1, TOK), jnp.int32),
            pltpu.VMEM((2 * WINDOW, 2 * FIELDS), low_type),
            pltpu.VMEM((2, 2 * WINDOW, HEAD_DIM), full_type),
            pltpu.VMEM((heads, 2, WINDOW, HEAD_DIM), full_type),
            pltpu.VMEM((2 * WINDOW, HEAD_DIM), full_type),
            pltpu.VMEM((heads, 2, WINDOW, HEAD_DIM), low_type),
            pltpu.VMEM((heads, 2, WINDOW, HEAD_DIM), low_type),
            pltpu.VMEM((heads, 3, WINDOW, HEAD_DIM), low_type),
            dma,
            dma,
            dma,
            dma,
            dma((heads,)),
            dma((heads,)),
            dma((heads,)),
            dma((heads,)),
            dma((heads,)),
            dma((heads,)),
            dma((heads,)),
            dma((heads,)),
            dma((heads,)),
            dma((heads,)),
            dma((3,)),
            dma,
            dma,
            dma,
            dma,
        ],
        compiler_params=pltpu.CompilerParams(
            collective_id=0, has_side_effects=True, vmem_limit_bytes=60 * 2**20
        ),
    )(lengths, field_bias, fields, queries[0], keys[0], values[0], grad_out[0])
    results = (query_grad, key_grad, value_grad, bias_total)
    query_grad, key_grad, value_grad, bias_total = pl.pallas_call(
        copy_kernel,
        out_shape=tuple(jax.ShapeDtypeStruct(one.shape, one.dtype) for one in results),
        in_specs=[in_vmem] * 4,
        out_specs=(in_hbm,) * 4,
        scratch_shapes=[dma((4,))],
        compiler_params=pltpu.CompilerParams(vmem_limit_bytes=2**20),
    )(*results)
    return query_grad[None], key_grad[None], value_grad[None], bias_total


def solution(mesh):
    rows = P("dp", "seq", None)
    return jax.shard_map(
        functools.partial(shards, mesh.shape["seq"] // GROUP, mesh.shape["dp"]),
        mesh=mesh,
        in_specs=(rows, rows, rows, rows, P("dp"), P("dp", "seq"), P()),
        out_specs=(rows, rows, rows, P()),
        check_vma=False,
    )
```

```python
import functools

import jax
import jax.numpy as jnp
from jax import lax
from jax.experimental import pallas as pl
from jax.experimental.pallas import tpu as pltpu
from jax.sharding import PartitionSpec as P

HEADS = 16
HEAD_DIM = 128
WINDOW = 512
FIELDS = 64
TOK = 128
GROUP = WINDOW // TOK
LOCAL_HEADS = HEADS // GROUP
SCALE = HEAD_DIM**-0.5
LOG2E = 1.4426950408889634
MASKED = -1e30
NT = (((1,), (1,)), ((), ()))
NN = (((1,), (0,)), ((), ()))
TN = (((0,), (0,)), ((), ()))


def dot(lhs, rhs, dims):
    return lax.dot_general(lhs, rhs, dims, preferred_element_type=jnp.float32)


def kernel(
    planes,
    copies,
    length_ref,
    bias_ref,
    fields_ref,
    q_hbm,
    k_hbm,
    v_hbm,
    g_hbm,
    dq_ref,
    dk_ref,
    dv_ref,
    dbias_ref,
    bias_rows,
    bias_part,
    mine,
    plane_parts,
    mate_parts,
    kv,
    qg,
    field_rows,
    onehot,
    key_acc,
    own_acc,
    col_acc,
    ret_src,
    ret_dst,
    out_buf,
    field_send,
    field_recv,
    field_relay,
    field_halo,
    kv_send,
    kv_recv,
    qg_send,
    qg_recv,
    halo_send,
    halo_recv,
    ret_send,
    ret_recv,
    outq_send,
    outkv_send,
    out_recv,
    plane_send,
    plane_recv,
    mate_send,
    mate_recv,
    rows_ready,
    known,
):
    block = lax.axis_index("seq")
    sequence = lax.axis_index("dp")
    y = lax.rem(block, GROUP)
    z = block // GROUP
    has_prev = z > 0
    has_next = z < planes - 1

    def peer(step):
        other = lax.rem(y + step, GROUP)
        return other, {"seq": z * GROUP + other}

    nxt = {"seq": block + GROUP}
    prv = {"seq": block - GROUP}

    mates = copies * GROUP
    seat = sequence * GROUP + y

    def at_distance(distance, act):
        @pl.when(z >= distance)
        def _():
            act(block - distance * GROUP)

        @pl.when(z + distance < planes)
        def _():
            act(block + distance * GROUP)

    def count_at(distance):
        below = (z >= distance).astype(jnp.int32)
        return below + (z + distance < planes).astype(jnp.int32)

    barrier = pltpu.get_barrier_semaphore()

    def greet(other):
        pl.semaphore_signal(barrier, inc=1, device_id={"seq": other})

    def twin(step):
        return {"dp": lax.rem(sequence + step, copies)}

    for step in range(1, GROUP):
        pl.semaphore_signal(barrier, inc=1, device_id=peer(step)[1])
    at_distance(1, greet)
    for step in range(1, copies):
        pl.semaphore_signal(barrier, inc=1, device_id=twin(step))
    own_rows = pl.ds(pl.multiple_of(y * TOK, TOK), TOK)
    own_keys = pl.ds(pl.multiple_of(WINDOW + y * TOK, TOK), TOK)
    plane_keys = pl.ds(WINDOW, WINDOW)

    def columns(owner, head):
        return pl.ds(pl.multiple_of((owner * LOCAL_HEADS + head) * HEAD_DIM, HEAD_DIM), HEAD_DIM)

    arrays = ((kv_send, kv_recv, (k_hbm, v_hbm), kv, own_keys), (qg_send, qg_recv, (q_hbm, g_hbm), qg, own_rows))

    pltpu.make_async_copy(fields_ref, field_rows.at[GROUP + y], field_recv).start()
    for head in range(LOCAL_HEADS):
        for _, recv, sources, target, rows in arrays:
            for index, source in enumerate(sources):
                pltpu.make_async_copy(
                    source.at[:, columns(y, head)], target.at[head, index, rows], recv.at[head, y]
                ).start()

    pl.semaphore_wait(barrier, GROUP + copies - 2 + count_at(1))

    def give(kind, head):
        send, recv, sources, target, rows = arrays[kind]
        for step in range(1, GROUP):
            other, device = peer(step)
            for index, source in enumerate(sources):
                pltpu.make_async_remote_copy(
                    source.at[:, columns(other, head)],
                    target.at[head, index, rows],
                    send.at[head],
                    recv.at[head, y],
                    device_id=device,
                ).start()

    give(0, 0)

    @pl.when(has_next)
    def _():
        for head in range(LOCAL_HEADS):
            for index, source in enumerate((k_hbm, v_hbm)):
                pltpu.make_async_remote_copy(
                    source.at[:, columns(y, head)],
                    kv.at[head, index, own_rows],
                    halo_send.at[head],
                    halo_recv.at[head, y],
                    device_id=nxt,
                ).start()

    for step in range(1, GROUP):
        pltpu.make_async_remote_copy(
            fields_ref, field_rows.at[GROUP + y], field_send, field_recv, device_id=peer(step)[1]
        ).start()
    give(0, 1)
    give(1, 0)

    for step in range(1, copies):
        pl.semaphore_signal(rows_ready, inc=1, device_id=twin(step))

    def tell(turn):
        def act(other):
            pl.semaphore_signal(known.at[turn], inc=1, device_id={"seq": other})

        at_distance(2**turn, act)

    def hear(turn):
        pl.semaphore_wait(known.at[turn], count_at(2**turn))

    turns = (planes - 1).bit_length()
    tell(0)

    @pl.when(jnp.logical_not(has_prev))
    def _():
        kv[:, :, 0:WINDOW, :] = jnp.zeros((LOCAL_HEADS, 2, WINDOW, HEAD_DIM), kv.dtype)
        field_rows[0:GROUP] = jnp.full((GROUP, 1, TOK), -1, jnp.int32)

    plane_fields = field_rows.at[pl.ds(GROUP, GROUP)]
    halo_fields = field_rows.at[pl.ds(0, GROUP)]
    pltpu.make_async_copy(plane_fields, plane_fields, field_recv).wait()

    @pl.when(has_next)
    def _():
        pltpu.make_async_remote_copy(
            plane_fields, halo_fields, field_relay, field_halo, device_id=nxt
        ).start()

    def block_rows(first, source):
        return pl.ds(pl.multiple_of(first + source * TOK, TOK), TOK)

    def relay(head):
        own = kv.at[head, :, own_keys]
        pltpu.make_async_copy(own, own, kv_recv.at[head, y]).wait()
        for step in range(1, GROUP):
            source = lax.rem(y + GROUP - step, GROUP)
            arrived = kv.at[head, :, block_rows(WINDOW, source)]
            pltpu.make_async_copy(arrived, arrived, kv_recv.at[head, source]).wait()

            @pl.when(has_next)
            def _():
                pltpu.make_async_remote_copy(
                    arrived,
                    kv.at[head, :, block_rows(0, source)],
                    halo_send.at[head],
                    halo_recv.at[head, source],
                    device_id=nxt,
                ).start()

    relay(0)
    give(0, 2)

    @pl.when(has_prev)
    def _():
        pltpu.make_async_copy(halo_fields, halo_fields, field_halo).wait()

    lane = lax.broadcasted_iota(jnp.int32, (TOK, TOK), 1)
    row = lax.broadcasted_iota(jnp.int32, (TOK, TOK), 0)
    for part in range(2 * GROUP):
        by_lane = jnp.broadcast_to(field_rows[part].astype(jnp.float32), (TOK, TOK))
        by_row = by_lane.T
        chosen = by_row == lax.rem(lane, FIELDS).astype(jnp.float32)
        onehot[part * TOK : (part + 1) * TOK] = chosen.astype(jnp.float32).astype(jnp.bfloat16)

    field = lax.broadcasted_iota(jnp.int32, (FIELDS, 2 * FIELDS), 0)
    place = lax.broadcasted_iota(jnp.int32, (FIELDS, 2 * FIELDS), 1)
    twice = (lax.rem(place, FIELDS) == field).astype(jnp.float32).astype(jnp.bfloat16)
    scaled = dot(bias_ref[...], twice, NN) / SCALE
    high_part = scaled.astype(jnp.bfloat16).astype(jnp.float32)
    is_high = lax.broadcasted_iota(jnp.int32, (HEADS, 2 * FIELDS), 1) < FIELDS
    bias_rows[...] = jnp.where(is_high, high_part, scaled - high_part)

    older = row > lane
    length = length_ref[0]
    unseen = jnp.where(has_prev, 0.0, MASKED)

    def work(head):
        @pl.when(has_prev)
        def _():
            for source in range(GROUP):
                halo = kv.at[head, :, pl.ds(source * TOK, TOK)]
                pltpu.make_async_copy(halo, halo, halo_recv.at[head, source]).wait()

        bias_row = bias_rows[pl.ds(y * LOCAL_HEADS + head, 1), :]
        bias_block = jnp.broadcast_to(bias_row, (TOK, TOK)).astype(jnp.bfloat16)
        for part in range(GROUP):
            first = part * TOK
            span = WINDOW + TOK
            seen = pl.ds(first, span)
            here = qg.at[head, :, pl.ds(first, TOK)]
            pltpu.make_async_copy(here, here, qg_recv.at[head, part]).wait()
            queries = qg[head, 0, first : first + TOK, :]
            grads = qg[head, 1, first : first + TOK, :]
            keys = kv[head, 0, seen, :]
            values = kv[head, 1, seen, :]
            logits = dot(
                jnp.concatenate([keys, onehot[seen, :]], axis=1),
                jnp.concatenate([queries, bias_block], axis=1),
                NT,
            )
            probs_grad = dot(values, grads, NT)

            def tiles(full):
                merged = jnp.where(older, full[0:TOK], full[WINDOW:span])
                return [merged] + [full[t * TOK : (t + 1) * TOK] for t in range(1, GROUP)]

            logit_tiles = tiles(logits)
            halo_tiles = GROUP - part
            logit_tiles = [
                (jnp.where(older, tile + unseen, tile) if t == 0 else tile + unseen)
                if t < halo_tiles
                else tile
                for t, tile in enumerate(logit_tiles)
            ]
            logit = jnp.concatenate(logit_tiles, axis=0)
            peak = jnp.max(logit, axis=0, keepdims=True)
            power = jnp.exp2((logit - peak) * (SCALE * LOG2E))
            total = jnp.sum(power, axis=0, keepdims=True)
            place = z * WINDOW + first + lax.broadcasted_iota(jnp.int32, (1, TOK), 1)
            share = jnp.where(place < length, 1.0 / total, 0.0)
            weight = power * share
            weight_low = weight.astype(jnp.bfloat16)
            prob = jnp.concatenate(tiles(probs_grad), axis=0)
            delta = jnp.sum(weight_low.astype(jnp.float32) * prob, axis=0, keepdims=True)
            grad = weight * (prob - delta)

            def spread(merged):
                top = merged[0:TOK]
                none = jnp.zeros_like(top)
                return jnp.concatenate(
                    [jnp.where(older, top, none), merged[TOK:WINDOW], jnp.where(older, none, top)],
                    axis=0,
                )

            grad_full = spread(grad)
            grad_low = grad_full.astype(jnp.bfloat16)
            weight_full = spread(weight_low.astype(jnp.float32)).astype(jnp.bfloat16)
            query_grad = dot(grad_low, keys, TN) * SCALE
            out_buf[head, 0, first : first + TOK, :] = query_grad.astype(jnp.bfloat16)
            key_part = dot(grad_low, queries, NN)
            value_part = dot(weight_full, grads, NN)
            for store, fresh in ((key_acc.at[0], key_part), (key_acc.at[1], value_part), (col_acc, grad_full)):
                if part == 0:
                    store[0:span, :] = fresh
                else:
                    store[first : first + WINDOW, :] += fresh[0:WINDOW]
                    store[first + WINDOW : first + span, :] = fresh[WINDOW:span]

        own_acc[head, 0] = key_acc[0, WINDOW:] * SCALE
        own_acc[head, 1] = key_acc[1, WINDOW:]


        sums = col_acc[...]
        high = sums.astype(jnp.bfloat16)
        low = (sums - high.astype(jnp.float32)).astype(jnp.bfloat16)
        by_query = dot(high, onehot[...], TN) + dot(low, onehot[...], TN)
        bias_part[head] = jnp.sum(by_query, axis=0, keepdims=True)

    def give_back(head):
        ret_src[head, 0] = (key_acc[0, 0:WINDOW] * SCALE).astype(jnp.bfloat16)
        ret_src[head, 1] = key_acc[1, 0:WINDOW].astype(jnp.bfloat16)

        @pl.when(has_prev)
        def _():
            pltpu.make_async_remote_copy(
                ret_src.at[head],
                ret_dst.at[head],
                ret_send.at[head],
                ret_recv.at[head],
                device_id=prv,
            ).start()

    def give_query(head):
        for step in range(1, GROUP):
            other, device = peer(step)
            pltpu.make_async_remote_copy(
                out_buf.at[head, 0, pl.ds(pl.multiple_of(other * TOK, TOK), TOK)],
                dq_ref.at[:, columns(y, head)],
                outq_send.at[head],
                out_recv.at[0],
                device_id=device,
            ).start()
        pltpu.make_async_copy(
            out_buf.at[head, 0, own_rows], dq_ref.at[:, columns(y, head)], out_recv.at[0]
        ).start()

    def finish(head):
        @pl.when(has_next)
        def _():
            back = ret_dst.at[head]
            pltpu.make_async_copy(back, back, ret_recv.at[head]).wait()
            for index in range(2):
                out_buf[head, 1 + index] = (
                    own_acc[head, index] + ret_dst[head, index].astype(jnp.float32)
                ).astype(jnp.bfloat16)

        @pl.when(jnp.logical_not(has_next))
        def _():
            for index in range(2):
                out_buf[head, 1 + index] = own_acc[head, index].astype(jnp.bfloat16)

        for index, result in ((1, dk_ref), (2, dv_ref)):
            for step in range(1, GROUP):
                other, device = peer(step)
                pltpu.make_async_remote_copy(
                    out_buf.at[head, index, pl.ds(pl.multiple_of(other * TOK, TOK), TOK)],
                    result.at[:, columns(y, head)],
                    outkv_send.at[head],
                    out_recv.at[index],
                    device_id=device,
                ).start()
            pltpu.make_async_copy(
                out_buf.at[head, index, own_rows], result.at[:, columns(y, head)], out_recv.at[index]
            ).start()

    hear(0)
    tell(1)
    relay(1)
    give(0, 3)
    give(1, 1)

    @pl.loop(0, LOCAL_HEADS)
    def _(head):
        for turn in range(1, turns - 1):

            @pl.when(head == min(turn - 1, LOCAL_HEADS - 1))
            def _():
                hear(turn)
                tell(turn + 1)

        work(head)

        @pl.when(head == 0)
        def _():
            for later in range(2, LOCAL_HEADS):
                relay(later)
                give(1, later)

        @pl.when(head == LOCAL_HEADS - 1)
        def _():
            for pair in range(LOCAL_HEADS // 2):
                mine[pair] = jnp.where(is_high[0:1], bias_part[2 * pair], bias_part[2 * pair + 1])
            plane_parts[z] = mine[...]
            hear(turns - 1)

            @pl.loop(0, planes - 1)
            def _(step):
                target = step + (step >= z).astype(jnp.int32)
                pltpu.make_async_remote_copy(
                    mine,
                    plane_parts.at[z],
                    plane_send,
                    plane_recv,
                    device_id={"seq": target * GROUP + y},
                ).start()

        give_back(head)

    def rest_of(parts):
        return parts.at[pl.ds(0, parts.shape[0] - 1)]

    def landed(parts, sem):
        pltpu.make_async_copy(rest_of(parts), rest_of(parts), sem).wait()

    def sum_of(parts):
        total = parts[0]
        for index in range(1, parts.shape[0]):
            total = total + parts[index]
        return total

    for head in range(LOCAL_HEADS):
        give_query(head)
        finish(head)

    landed(plane_parts, plane_recv)
    mate_parts[seat] = sum_of(plane_parts)
    pl.semaphore_wait(rows_ready, copies - 1)

    @pl.loop(1, mates)
    def _(step):
        other = lax.rem(seat + step, mates)
        part = mate_parts.at[seat]
        pltpu.make_async_remote_copy(
            part,
            part,
            mate_send,
            mate_recv,
            device_id={"seq": z * GROUP + lax.rem(other, GROUP), "dp": other // GROUP},
        ).start()

    for parts, sem in ((plane_parts, plane_send), (mate_parts, mate_send)):
        landed(parts, sem)
    sent_fields = field_rows.at[pl.ds(0, GROUP - 1)]
    pltpu.make_async_copy(sent_fields, sent_fields, field_send).wait()

    @pl.when(has_next)
    def _():
        pltpu.make_async_copy(halo_fields, halo_fields, field_relay).wait()

    @pl.loop(0, LOCAL_HEADS)
    def _(head):
        sent = kv.at[head, :, pl.ds(0, WINDOW - TOK)]
        pltpu.make_async_copy(sent, sent, kv_send.at[head]).wait()
        pltpu.make_async_copy(sent, sent, qg_send.at[head]).wait()
        pltpu.make_async_copy(sent, sent, outkv_send.at[head]).wait()
        query_sent = kv.at[head, 0, pl.ds(0, WINDOW - TOK)]
        pltpu.make_async_copy(query_sent, query_sent, outq_send.at[head]).wait()

        @pl.when(has_next)
        def _():
            halo = kv.at[head, :, pl.ds(0, WINDOW)]
            pltpu.make_async_copy(halo, halo, halo_send.at[head]).wait()

        @pl.when(has_prev)
        def _():
            source = ret_src.at[head]
            pltpu.make_async_copy(source, source, ret_send.at[head]).wait()

    for index, result in enumerate((dq_ref, dk_ref, dv_ref)):
        pltpu.make_async_copy(result, result, out_recv.at[index]).wait()

    landed(mate_parts, mate_recv)
    for owner in range(GROUP):
        for pair in range(LOCAL_HEADS // 2):
            both = mate_parts[owner, pair]
            for copy in range(1, copies):
                both = both + mate_parts[copy * GROUP + owner, pair]
            first = owner * LOCAL_HEADS + 2 * pair
            dbias_ref[first : first + 1, :] = both[:, 0:FIELDS]
            dbias_ref[first + 1 : first + 2, :] = pltpu.roll(both, FIELDS, 1)[:, 0:FIELDS]


def copy_kernel(*refs):
    count = len(refs) // 2
    sources, targets, sems = refs[:count], refs[count : 2 * count], refs[-1]
    moves = [
        pltpu.make_async_copy(sources[index], targets[index], sems.at[index]) for index in range(count)
    ]
    for move in moves:
        move.start()
    for move in moves:
        move.wait()


def shards(planes, copies, queries, keys, values, grad_out, lengths, fields, field_bias):
    tok_rows, row_width = queries.shape[1:]
    low_type, full_type = jnp.bfloat16, jnp.float32
    grads_shape = jax.ShapeDtypeStruct((tok_rows, row_width), low_type)
    in_hbm = pl.BlockSpec(memory_space=pltpu.HBM)
    in_vmem = pl.BlockSpec(memory_space=pltpu.VMEM)
    dma = pltpu.SemaphoreType.DMA
    heads = LOCAL_HEADS
    query_grad, key_grad, value_grad, bias_total = pl.pallas_call(
        functools.partial(kernel, planes, copies),
        out_shape=(
            pltpu.VMEM(grads_shape.shape, low_type),
            pltpu.VMEM(grads_shape.shape, low_type),
            pltpu.VMEM(grads_shape.shape, low_type),
            pltpu.VMEM((HEADS, FIELDS), full_type),
        ),
        in_specs=[
            pl.BlockSpec(memory_space=pltpu.SMEM),
            in_vmem,
            in_vmem,
            in_hbm,
            in_hbm,
            in_hbm,
            in_hbm,
        ],
        out_specs=(in_vmem, in_vmem, in_vmem, in_vmem),
        scratch_shapes=[
            pltpu.VMEM((HEADS, 2 * FIELDS), full_type),
            pltpu.VMEM((heads, 1, 2 * FIELDS), full_type),
            pltpu.VMEM((heads // 2, 1, 2 * FIELDS), full_type),
            pltpu.VMEM((planes, heads // 2, 1, 2 * FIELDS), full_type),
            pltpu.VMEM((copies * GROUP, heads // 2, 1, 2 * FIELDS), full_type),
            pltpu.VMEM((heads, 2, 2 * WINDOW, HEAD_DIM), low_type),
            pltpu.VMEM((heads, 2, WINDOW, HEAD_DIM), low_type),
            pltpu.VMEM((2 * GROUP, 1, TOK), jnp.int32),
            pltpu.VMEM((2 * WINDOW, 2 * FIELDS), low_type),
            pltpu.VMEM((2, 2 * WINDOW, HEAD_DIM), full_type),
            pltpu.VMEM((heads, 2, WINDOW, HEAD_DIM), full_type),
            pltpu.VMEM((2 * WINDOW, HEAD_DIM), full_type),
            pltpu.VMEM((heads, 2, WINDOW, HEAD_DIM), low_type),
            pltpu.VMEM((heads, 2, WINDOW, HEAD_DIM), low_type),
            pltpu.VMEM((heads, 3, WINDOW, HEAD_DIM), low_type),
            dma,
            dma,
            dma,
            dma,
            dma((heads,)),
            dma((heads, GROUP)),
            dma((heads,)),
            dma((heads, GROUP)),
            dma((heads,)),
            dma((heads, GROUP)),
            dma((heads,)),
            dma((heads,)),
            dma((heads,)),
            dma((heads,)),
            dma((3,)),
            dma,
            dma,
            dma,
            dma,
            pltpu.SemaphoreType.REGULAR,
            pltpu.SemaphoreType.REGULAR(((planes - 1).bit_length(),)),
        ],
        compiler_params=pltpu.CompilerParams(
            collective_id=0, has_side_effects=True, vmem_limit_bytes=60 * 2**20
        ),
    )(lengths, field_bias, fields, queries[0], keys[0], values[0], grad_out[0])
    results = (query_grad, key_grad, value_grad, bias_total)
    query_grad, key_grad, value_grad, bias_total = pl.pallas_call(
        copy_kernel,
        out_shape=tuple(jax.ShapeDtypeStruct(one.shape, one.dtype) for one in results),
        in_specs=[in_vmem] * 4,
        out_specs=(in_hbm,) * 4,
        scratch_shapes=[dma((4,))],
        compiler_params=pltpu.CompilerParams(vmem_limit_bytes=2**20),
    )(*results)
    return query_grad[None], key_grad[None], value_grad[None], bias_total


def solution(mesh):
    rows = P("dp", "seq", None)
    return jax.shard_map(
        functools.partial(shards, mesh.shape["seq"] // GROUP, mesh.shape["dp"]),
        mesh=mesh,
        in_specs=(rows, rows, rows, rows, P("dp"), P("dp", "seq"), P()),
        out_specs=(rows, rows, rows, P()),
        check_vma=False,
    )
```

```python
import functools

import jax
import jax.numpy as jnp
from jax import lax
from jax.experimental import pallas as pl
from jax.experimental.pallas import tpu as pltpu
from jax.sharding import PartitionSpec as P

HEADS = 16
HEAD_DIM = 128
WINDOW = 512
FIELDS = 64
TOK = 128
GROUP = WINDOW // TOK
LOCAL_HEADS = HEADS // GROUP
SCALE = HEAD_DIM**-0.5
LOG2E = 1.4426950408889634
MASKED = -1e30
NT = (((1,), (1,)), ((), ()))
NN = (((1,), (0,)), ((), ()))
TN = (((0,), (0,)), ((), ()))


def dot(lhs, rhs, dims):
    return lax.dot_general(lhs, rhs, dims, preferred_element_type=jnp.float32)


def kernel(
    planes,
    copies,
    length_ref,
    bias_ref,
    fields_ref,
    q_hbm,
    k_hbm,
    v_hbm,
    g_hbm,
    dq_ref,
    dk_ref,
    dv_ref,
    dbias_ref,
    bias_rows,
    bias_part,
    mine,
    plane_parts,
    mate_parts,
    kv,
    qg,
    field_rows,
    onehot,
    field_of_key,
    key_acc,
    own_acc,
    col_acc,
    ret_src,
    ret_dst,
    out_buf,
    field_send,
    field_recv,
    field_relay,
    field_halo,
    kv_send,
    kv_recv,
    qg_send,
    qg_recv,
    halo_send,
    halo_recv,
    ret_send,
    ret_recv,
    outq_send,
    outkv_send,
    out_recv,
    plane_send,
    plane_recv,
    mate_send,
    mate_recv,
    rows_ready,
    known,
):
    block = lax.axis_index("seq")
    sequence = lax.axis_index("dp")
    y = lax.rem(block, GROUP)
    z = block // GROUP
    has_prev = z > 0
    has_next = z < planes - 1

    def peer(step):
        other = lax.rem(y + step, GROUP)
        return other, {"seq": z * GROUP + other}

    nxt = {"seq": block + GROUP}
    prv = {"seq": block - GROUP}

    mates = copies * GROUP
    seat = sequence * GROUP + y

    def at_distance(distance, act):
        @pl.when(z >= distance)
        def _():
            act(block - distance * GROUP)

        @pl.when(z + distance < planes)
        def _():
            act(block + distance * GROUP)

    def count_at(distance):
        below = (z >= distance).astype(jnp.int32)
        return below + (z + distance < planes).astype(jnp.int32)

    barrier = pltpu.get_barrier_semaphore()

    def greet(other):
        pl.semaphore_signal(barrier, inc=1, device_id={"seq": other})

    def twin(step):
        return {"dp": lax.rem(sequence + step, copies)}

    for step in range(1, GROUP):
        pl.semaphore_signal(barrier, inc=1, device_id=peer(step)[1])
    at_distance(1, greet)
    for step in range(1, copies):
        pl.semaphore_signal(barrier, inc=1, device_id=twin(step))
    own_rows = pl.ds(pl.multiple_of(y * TOK, TOK), TOK)
    own_keys = pl.ds(pl.multiple_of(WINDOW + y * TOK, TOK), TOK)
    plane_keys = pl.ds(WINDOW, WINDOW)

    def columns(owner, head):
        return pl.ds(pl.multiple_of((owner * LOCAL_HEADS + head) * HEAD_DIM, HEAD_DIM), HEAD_DIM)

    arrays = ((kv_send, kv_recv, (k_hbm, v_hbm), kv, own_keys), (qg_send, qg_recv, (q_hbm, g_hbm), qg, own_rows))

    pltpu.make_async_copy(fields_ref, field_rows.at[GROUP + y], field_recv).start()
    for head in range(LOCAL_HEADS):
        for _, recv, sources, target, rows in arrays:
            for index, source in enumerate(sources):
                pltpu.make_async_copy(
                    source.at[:, columns(y, head)], target.at[head, index, rows], recv.at[head, y]
                ).start()

    pl.semaphore_wait(barrier, GROUP + copies - 2 + count_at(1))

    def give(kind, head):
        send, recv, sources, target, rows = arrays[kind]
        for step in range(1, GROUP):
            other, device = peer(step)
            for index, source in enumerate(sources):
                pltpu.make_async_remote_copy(
                    source.at[:, columns(other, head)],
                    target.at[head, index, rows],
                    send.at[head],
                    recv.at[head, y],
                    device_id=device,
                ).start()

    give(0, 0)

    @pl.when(has_next)
    def _():
        for head in range(LOCAL_HEADS):
            for index, source in enumerate((k_hbm, v_hbm)):
                pltpu.make_async_remote_copy(
                    source.at[:, columns(y, head)],
                    kv.at[head, index, own_rows],
                    halo_send.at[head],
                    halo_recv.at[head, y],
                    device_id=nxt,
                ).start()

    for step in range(1, GROUP):
        pltpu.make_async_remote_copy(
            fields_ref, field_rows.at[GROUP + y], field_send, field_recv, device_id=peer(step)[1]
        ).start()
    give(0, 1)
    give(1, 0)

    for step in range(1, copies):
        pl.semaphore_signal(rows_ready, inc=1, device_id=twin(step))

    def tell(turn):
        def act(other):
            pl.semaphore_signal(known.at[turn], inc=1, device_id={"seq": other})

        at_distance(2**turn, act)

    def hear(turn):
        pl.semaphore_wait(known.at[turn], count_at(2**turn))

    turns = (planes - 1).bit_length()
    tell(0)

    @pl.when(jnp.logical_not(has_prev))
    def _():
        kv[:, :, 0:WINDOW, :] = jnp.zeros((LOCAL_HEADS, 2, WINDOW, HEAD_DIM), kv.dtype)
        field_rows[0:GROUP] = jnp.full((GROUP, 1, TOK), -1, jnp.int32)

    plane_fields = field_rows.at[pl.ds(GROUP, GROUP)]
    halo_fields = field_rows.at[pl.ds(0, GROUP)]
    pltpu.make_async_copy(plane_fields, plane_fields, field_recv).wait()

    @pl.when(has_next)
    def _():
        pltpu.make_async_remote_copy(
            plane_fields, halo_fields, field_relay, field_halo, device_id=nxt
        ).start()

    def block_rows(first, source):
        return pl.ds(pl.multiple_of(first + source * TOK, TOK), TOK)

    def relay(head):
        own = kv.at[head, :, own_keys]
        pltpu.make_async_copy(own, own, kv_recv.at[head, y]).wait()
        for step in range(1, GROUP):
            source = lax.rem(y + GROUP - step, GROUP)
            arrived = kv.at[head, :, block_rows(WINDOW, source)]
            pltpu.make_async_copy(arrived, arrived, kv_recv.at[head, source]).wait()

            @pl.when(has_next)
            def _():
                pltpu.make_async_remote_copy(
                    arrived,
                    kv.at[head, :, block_rows(0, source)],
                    halo_send.at[head],
                    halo_recv.at[head, source],
                    device_id=nxt,
                ).start()

    relay(0)
    give(0, 2)

    @pl.when(has_prev)
    def _():
        pltpu.make_async_copy(halo_fields, halo_fields, field_halo).wait()

    lane = lax.broadcasted_iota(jnp.int32, (TOK, TOK), 1)
    row = lax.broadcasted_iota(jnp.int32, (TOK, TOK), 0)
    for part in range(2 * GROUP):
        by_lane = jnp.broadcast_to(field_rows[part].astype(jnp.float32), (TOK, TOK))
        by_row = by_lane.T
        by_field = by_lane == lax.rem(row, FIELDS).astype(jnp.float32)
        field_of_key[:, part * TOK : (part + 1) * TOK] = by_field.astype(jnp.float32).astype(jnp.bfloat16)
        chosen = by_row == lax.rem(lane, FIELDS).astype(jnp.float32)
        onehot[part * TOK : (part + 1) * TOK] = chosen.astype(jnp.float32).astype(jnp.bfloat16)

    field = lax.broadcasted_iota(jnp.int32, (FIELDS, 2 * FIELDS), 0)
    place = lax.broadcasted_iota(jnp.int32, (FIELDS, 2 * FIELDS), 1)
    twice = (lax.rem(place, FIELDS) == field).astype(jnp.float32).astype(jnp.bfloat16)
    scaled = dot(bias_ref[...], twice, NN) / SCALE
    high_part = scaled.astype(jnp.bfloat16).astype(jnp.float32)
    is_high = lax.broadcasted_iota(jnp.int32, (HEADS, 2 * FIELDS), 1) < FIELDS
    bias_rows[...] = jnp.where(is_high, high_part, scaled - high_part)

    older = row > lane
    older_low = older.astype(jnp.float32).astype(jnp.bfloat16)
    newer_low = 1.0 - older_low
    length = length_ref[0]
    unseen = jnp.where(has_prev, 0.0, MASKED)

    def work(head):
        for source in range(GROUP):
            here = qg.at[head, :, pl.ds(source * TOK, TOK)]
            pltpu.make_async_copy(here, here, qg_recv.at[head, source]).wait()

        @pl.when(has_prev)
        def _():
            for source in range(GROUP):
                halo = kv.at[head, :, pl.ds(source * TOK, TOK)]
                pltpu.make_async_copy(halo, halo, halo_recv.at[head, source]).wait()

        bias_row = bias_rows[pl.ds(y * LOCAL_HEADS + head, 1), :]
        bias_block = jnp.broadcast_to(bias_row, (TOK, TOK)).astype(jnp.bfloat16)
        for part in range(GROUP):
            first = part * TOK
            span = WINDOW + TOK
            seen = pl.ds(first, span)
            queries = qg[head, 0, first : first + TOK, :]
            grads = qg[head, 1, first : first + TOK, :]
            keys = kv[head, 0, seen, :]
            values = kv[head, 1, seen, :]
            logits = dot(
                jnp.concatenate([keys, onehot[seen, :]], axis=1),
                jnp.concatenate([queries, bias_block], axis=1),
                NT,
            )
            probs_grad = dot(values, grads, NT)

            def tiles(full):
                merged = jnp.where(older, full[0:TOK], full[WINDOW:span])
                return [merged] + [full[t * TOK : (t + 1) * TOK] for t in range(1, GROUP)]

            logit_tiles = tiles(logits)
            halo_tiles = GROUP - part
            logit_tiles = [
                (jnp.where(older, tile + unseen, tile) if t == 0 else tile + unseen)
                if t < halo_tiles
                else tile
                for t, tile in enumerate(logit_tiles)
            ]
            logit = jnp.concatenate(logit_tiles, axis=0)
            peak = jnp.max(logit, axis=0, keepdims=True)
            power = jnp.exp2((logit - peak) * (SCALE * LOG2E))
            total = jnp.sum(power, axis=0, keepdims=True)
            place = z * WINDOW + first + lax.broadcasted_iota(jnp.int32, (1, TOK), 1)
            share = jnp.where(place < length, 1.0 / total, 0.0)
            weight = power * share
            weight_low = weight.astype(jnp.bfloat16)
            prob = jnp.concatenate(tiles(probs_grad), axis=0)
            delta = jnp.sum(weight_low.astype(jnp.float32) * prob, axis=0, keepdims=True)
            grad = weight * (prob - delta)

            def spread(merged):
                top = merged[0:TOK]
                none = jnp.zeros_like(top)
                return jnp.concatenate(
                    [jnp.where(older, top, none), merged[TOK:WINDOW], jnp.where(older, none, top)],
                    axis=0,
                )

            def low_spread(merged):
                top = merged[0:TOK]
                return jnp.concatenate([top * older_low, merged[TOK:WINDOW], top * newer_low], axis=0)

            grad_full = spread(grad)
            grad_low = low_spread(grad.astype(jnp.bfloat16))
            weight_full = low_spread(weight_low)
            query_grad = dot(grad_low, keys, TN) * SCALE
            out_buf[head, 0, first : first + TOK, :] = query_grad.astype(jnp.bfloat16)
            key_part = dot(grad_low, queries, NN)
            value_part = dot(weight_full, grads, NN)
            for store, fresh in ((key_acc.at[0], key_part), (key_acc.at[1], value_part), (col_acc, grad_full)):
                if part == 0:
                    store[0:span, :] = fresh
                else:
                    store[first : first + WINDOW, :] += fresh[0:WINDOW]
                    store[first + WINDOW : first + span, :] = fresh[WINDOW:span]


        sums = col_acc[...]
        high = sums.astype(jnp.bfloat16)
        low = (sums - high.astype(jnp.float32)).astype(jnp.bfloat16)
        by_query = dot(field_of_key[...], high, NN) + dot(field_of_key[...], low, NN)
        bias_part[head] = jnp.sum(by_query.T, axis=0, keepdims=True)

    def give_back(head):
        ret_src[head, 0] = (key_acc[0, 0:WINDOW] * SCALE).astype(jnp.bfloat16)
        ret_src[head, 1] = key_acc[1, 0:WINDOW].astype(jnp.bfloat16)

        own_acc[head, 0] = key_acc[0, WINDOW:] * SCALE
        own_acc[head, 1] = key_acc[1, WINDOW:]

    def send_back(head):
        @pl.when(has_prev)
        def _():
            pltpu.make_async_remote_copy(
                ret_src.at[head],
                ret_dst.at[head],
                ret_send.at[head],
                ret_recv.at[head],
                device_id=prv,
            ).start()

    def give_query(head):
        for step in range(1, GROUP):
            other, device = peer(step)
            pltpu.make_async_remote_copy(
                out_buf.at[head, 0, pl.ds(pl.multiple_of(other * TOK, TOK), TOK)],
                dq_ref.at[:, columns(y, head)],
                outq_send.at[head],
                out_recv.at[0],
                device_id=device,
            ).start()
        pltpu.make_async_copy(
            out_buf.at[head, 0, own_rows], dq_ref.at[:, columns(y, head)], out_recv.at[0]
        ).start()

    def finish(head):
        @pl.when(has_next)
        def _():
            back = ret_dst.at[head]
            pltpu.make_async_copy(back, back, ret_recv.at[head]).wait()
            for index in range(2):
                out_buf[head, 1 + index] = (
                    own_acc[head, index] + ret_dst[head, index].astype(jnp.float32)
                ).astype(jnp.bfloat16)

        @pl.when(jnp.logical_not(has_next))
        def _():
            for index in range(2):
                out_buf[head, 1 + index] = own_acc[head, index].astype(jnp.bfloat16)

        for index, result in ((1, dk_ref), (2, dv_ref)):
            for step in range(1, GROUP):
                other, device = peer(step)
                pltpu.make_async_remote_copy(
                    out_buf.at[head, index, pl.ds(pl.multiple_of(other * TOK, TOK), TOK)],
                    result.at[:, columns(y, head)],
                    outkv_send.at[head],
                    out_recv.at[index],
                    device_id=device,
                ).start()
            pltpu.make_async_copy(
                out_buf.at[head, index, own_rows], result.at[:, columns(y, head)], out_recv.at[index]
            ).start()

    hear(0)
    tell(1)
    relay(1)
    give(0, 3)
    give(1, 1)

    @pl.loop(0, LOCAL_HEADS)
    def _(head):
        for turn in range(1, turns - 1):

            @pl.when(head == min(turn - 1, LOCAL_HEADS - 1))
            def _():
                hear(turn)
                tell(turn + 1)

        @pl.when(head == LOCAL_HEADS - 1)
        def _():
            for ready in range(LOCAL_HEADS - 1):
                give_query(ready)
            finish(0)

        work(head)

        @pl.when(head == 0)
        def _():
            for later in range(2, LOCAL_HEADS):
                relay(later)
                give(1, later)

        @pl.when(head == LOCAL_HEADS - 1)
        def _():
            for pair in range(LOCAL_HEADS // 2):
                mine[pair] = jnp.where(is_high[0:1], bias_part[2 * pair], bias_part[2 * pair + 1])
            plane_parts[z] = mine[...]
            hear(turns - 1)

            @pl.loop(0, planes - 1)
            def _(step):
                target = step + (step >= z).astype(jnp.int32)
                pltpu.make_async_remote_copy(
                    mine,
                    plane_parts.at[z],
                    plane_send,
                    plane_recv,
                    device_id={"seq": target * GROUP + y},
                ).start()

        give_back(head)

        @pl.when(head < LOCAL_HEADS - 2)
        def _():
            send_back(head)


    def rest_of(parts):
        return parts.at[pl.ds(0, parts.shape[0] - 1)]

    def landed(parts, sem):
        pltpu.make_async_copy(rest_of(parts), rest_of(parts), sem).wait()

    def sum_of(parts):
        total = parts[0]
        for index in range(1, parts.shape[0]):
            total = total + parts[index]
        return total

    send_back(LOCAL_HEADS - 2)
    send_back(LOCAL_HEADS - 1)
    give_query(LOCAL_HEADS - 1)
    for head in range(1, LOCAL_HEADS):
        finish(head)

    landed(plane_parts, plane_recv)
    mate_parts[seat] = sum_of(plane_parts)
    pl.semaphore_wait(rows_ready, copies - 1)

    @pl.loop(1, mates)
    def _(step):
        other = lax.rem(seat + step, mates)
        part = mate_parts.at[seat]
        pltpu.make_async_remote_copy(
            part,
            part,
            mate_send,
            mate_recv,
            device_id={"seq": z * GROUP + lax.rem(other, GROUP), "dp": other // GROUP},
        ).start()

    for parts, sem in ((plane_parts, plane_send), (mate_parts, mate_send)):
        landed(parts, sem)
    sent_fields = field_rows.at[pl.ds(0, GROUP - 1)]
    pltpu.make_async_copy(sent_fields, sent_fields, field_send).wait()

    @pl.when(has_next)
    def _():
        pltpu.make_async_copy(halo_fields, halo_fields, field_relay).wait()

    @pl.loop(0, LOCAL_HEADS)
    def _(head):
        sent = kv.at[head, :, pl.ds(0, WINDOW - TOK)]
        pltpu.make_async_copy(sent, sent, kv_send.at[head]).wait()
        pltpu.make_async_copy(sent, sent, qg_send.at[head]).wait()
        pltpu.make_async_copy(sent, sent, outkv_send.at[head]).wait()
        query_sent = kv.at[head, 0, pl.ds(0, WINDOW - TOK)]
        pltpu.make_async_copy(query_sent, query_sent, outq_send.at[head]).wait()

        @pl.when(has_next)
        def _():
            halo = kv.at[head, :, pl.ds(0, WINDOW)]
            pltpu.make_async_copy(halo, halo, halo_send.at[head]).wait()

        @pl.when(has_prev)
        def _():
            source = ret_src.at[head]
            pltpu.make_async_copy(source, source, ret_send.at[head]).wait()

    for index, result in enumerate((dq_ref, dk_ref, dv_ref)):
        pltpu.make_async_copy(result, result, out_recv.at[index]).wait()

    landed(mate_parts, mate_recv)
    for owner in range(GROUP):
        for pair in range(LOCAL_HEADS // 2):
            both = mate_parts[owner, pair]
            for copy in range(1, copies):
                both = both + mate_parts[copy * GROUP + owner, pair]
            first = owner * LOCAL_HEADS + 2 * pair
            dbias_ref[first : first + 1, :] = both[:, 0:FIELDS]
            dbias_ref[first + 1 : first + 2, :] = pltpu.roll(both, FIELDS, 1)[:, 0:FIELDS]


def copy_kernel(*refs):
    count = len(refs) // 2
    sources, targets, sems = refs[:count], refs[count : 2 * count], refs[-1]
    moves = [
        pltpu.make_async_copy(sources[index], targets[index], sems.at[index]) for index in range(count)
    ]
    for move in moves:
        move.start()
    for move in moves:
        move.wait()


def shards(planes, copies, queries, keys, values, grad_out, lengths, fields, field_bias):
    tok_rows, row_width = queries.shape[1:]
    low_type, full_type = jnp.bfloat16, jnp.float32
    grads_shape = jax.ShapeDtypeStruct((tok_rows, row_width), low_type)
    in_hbm = pl.BlockSpec(memory_space=pltpu.HBM)
    in_vmem = pl.BlockSpec(memory_space=pltpu.VMEM)
    dma = pltpu.SemaphoreType.DMA
    heads = LOCAL_HEADS
    query_grad, key_grad, value_grad, bias_total = pl.pallas_call(
        functools.partial(kernel, planes, copies),
        out_shape=(
            pltpu.VMEM(grads_shape.shape, low_type),
            pltpu.VMEM(grads_shape.shape, low_type),
            pltpu.VMEM(grads_shape.shape, low_type),
            pltpu.VMEM((HEADS, FIELDS), full_type),
        ),
        in_specs=[
            pl.BlockSpec(memory_space=pltpu.SMEM),
            in_vmem,
            in_vmem,
            in_hbm,
            in_hbm,
            in_hbm,
            in_hbm,
        ],
        out_specs=(in_vmem, in_vmem, in_vmem, in_vmem),
        scratch_shapes=[
            pltpu.VMEM((HEADS, 2 * FIELDS), full_type),
            pltpu.VMEM((heads, 1, 2 * FIELDS), full_type),
            pltpu.VMEM((heads // 2, 1, 2 * FIELDS), full_type),
            pltpu.VMEM((planes, heads // 2, 1, 2 * FIELDS), full_type),
            pltpu.VMEM((copies * GROUP, heads // 2, 1, 2 * FIELDS), full_type),
            pltpu.VMEM((heads, 2, 2 * WINDOW, HEAD_DIM), low_type),
            pltpu.VMEM((heads, 2, WINDOW, HEAD_DIM), low_type),
            pltpu.VMEM((2 * GROUP, 1, TOK), jnp.int32),
            pltpu.VMEM((2 * WINDOW, 2 * FIELDS), low_type),
            pltpu.VMEM((2 * FIELDS, 2 * WINDOW), low_type),
            pltpu.VMEM((2, 2 * WINDOW, HEAD_DIM), full_type),
            pltpu.VMEM((heads, 2, WINDOW, HEAD_DIM), full_type),
            pltpu.VMEM((2 * WINDOW, HEAD_DIM), full_type),
            pltpu.VMEM((heads, 2, WINDOW, HEAD_DIM), low_type),
            pltpu.VMEM((heads, 2, WINDOW, HEAD_DIM), low_type),
            pltpu.VMEM((heads, 3, WINDOW, HEAD_DIM), low_type),
            dma,
            dma,
            dma,
            dma,
            dma((heads,)),
            dma((heads, GROUP)),
            dma((heads,)),
            dma((heads, GROUP)),
            dma((heads,)),
            dma((heads, GROUP)),
            dma((heads,)),
            dma((heads,)),
            dma((heads,)),
            dma((heads,)),
            dma((3,)),
            dma,
            dma,
            dma,
            dma,
            pltpu.SemaphoreType.REGULAR,
            pltpu.SemaphoreType.REGULAR(((planes - 1).bit_length(),)),
        ],
        compiler_params=pltpu.CompilerParams(
            collective_id=0, has_side_effects=True, vmem_limit_bytes=60 * 2**20
        ),
    )(lengths, field_bias, fields, queries[0], keys[0], values[0], grad_out[0])
    results = (query_grad, key_grad, value_grad, bias_total)
    query_grad, key_grad, value_grad, bias_total = pl.pallas_call(
        copy_kernel,
        out_shape=tuple(jax.ShapeDtypeStruct(one.shape, one.dtype) for one in results),
        in_specs=[in_vmem] * 4,
        out_specs=(in_hbm,) * 4,
        scratch_shapes=[dma((4,))],
        compiler_params=pltpu.CompilerParams(vmem_limit_bytes=2**20),
    )(*results)
    return query_grad[None], key_grad[None], value_grad[None], bias_total


def solution(mesh):
    rows = P("dp", "seq", None)
    return jax.shard_map(
        functools.partial(shards, mesh.shape["seq"] // GROUP, mesh.shape["dp"]),
        mesh=mesh,
        in_specs=(rows, rows, rows, rows, P("dp"), P("dp", "seq"), P()),
        out_specs=(rows, rows, rows, P()),
        check_vma=False,
    )
```

```python
import functools

import jax
import jax.numpy as jnp
from jax import lax
from jax.experimental import pallas as pl
from jax.experimental.pallas import tpu as pltpu
from jax.sharding import PartitionSpec as P

HEADS = 16
HEAD_DIM = 128
WINDOW = 512
FIELDS = 64
TOK = 128
GROUP = WINDOW // TOK
LOCAL_HEADS = HEADS // GROUP
SCALE = HEAD_DIM**-0.5
LOG2E = 1.4426950408889634
MASKED = -1e30
NT = (((1,), (1,)), ((), ()))
NN = (((1,), (0,)), ((), ()))
TN = (((0,), (0,)), ((), ()))


def dot(lhs, rhs, dims):
    return lax.dot_general(lhs, rhs, dims, preferred_element_type=jnp.float32)


def kernel(
    planes,
    copies,
    length_ref,
    bias_ref,
    fields_ref,
    q_hbm,
    k_hbm,
    v_hbm,
    g_hbm,
    dq_ref,
    dk_ref,
    dv_ref,
    dbias_ref,
    bias_rows,
    bias_part,
    mine,
    plane_parts,
    mate_parts,
    kv,
    qg,
    field_rows,
    onehot,
    field_of_key,
    key_acc,
    own_acc,
    col_acc,
    ret_src,
    ret_dst,
    out_buf,
    field_send,
    field_recv,
    field_relay,
    field_halo,
    kv_send,
    kv_recv,
    qg_send,
    qg_recv,
    halo_send,
    halo_recv,
    ret_send,
    ret_recv,
    outq_send,
    outkv_send,
    out_recv,
    plane_send,
    plane_recv,
    mate_send,
    mate_recv,
    rows_ready,
    known,
):
    block = lax.axis_index("seq")
    sequence = lax.axis_index("dp")
    y = lax.rem(block, GROUP)
    z = block // GROUP
    has_prev = z > 0
    has_next = z < planes - 1

    def peer(step):
        other = lax.rem(y + step, GROUP)
        return other, {"seq": z * GROUP + other}

    nxt = {"seq": block + GROUP}
    prv = {"seq": block - GROUP}

    mates = copies * GROUP
    seat = sequence * GROUP + y

    def at_distance(distance, act):
        @pl.when(z >= distance)
        def _():
            act(block - distance * GROUP)

        @pl.when(z + distance < planes)
        def _():
            act(block + distance * GROUP)

    def count_at(distance):
        below = (z >= distance).astype(jnp.int32)
        return below + (z + distance < planes).astype(jnp.int32)

    barrier = pltpu.get_barrier_semaphore()

    def greet(other):
        pl.semaphore_signal(barrier, inc=1, device_id={"seq": other})

    def twin(step):
        return {"dp": lax.rem(sequence + step, copies)}

    for step in range(1, GROUP):
        pl.semaphore_signal(barrier, inc=1, device_id=peer(step)[1])
    at_distance(1, greet)
    for step in range(1, copies):
        pl.semaphore_signal(barrier, inc=1, device_id=twin(step))
    own_rows = pl.ds(pl.multiple_of(y * TOK, TOK), TOK)
    own_keys = pl.ds(pl.multiple_of(WINDOW + y * TOK, TOK), TOK)
    plane_keys = pl.ds(WINDOW, WINDOW)

    def columns(owner, head):
        return pl.ds(pl.multiple_of((owner * LOCAL_HEADS + head) * HEAD_DIM, HEAD_DIM), HEAD_DIM)

    arrays = ((kv_send, kv_recv, (k_hbm, v_hbm), kv, own_keys), (qg_send, qg_recv, (q_hbm, g_hbm), qg, own_rows))

    pltpu.make_async_copy(fields_ref, field_rows.at[GROUP + y], field_recv).start()
    for head in range(LOCAL_HEADS):
        for _, recv, sources, target, rows in arrays:
            for index, source in enumerate(sources):
                pltpu.make_async_copy(
                    source.at[:, columns(y, head)], target.at[head, index, rows], recv.at[head, y]
                ).start()

    pl.semaphore_wait(barrier, GROUP + copies - 2 + count_at(1))

    def give(kind, head):
        send, recv, sources, target, rows = arrays[kind]
        for step in range(1, GROUP):
            other, device = peer(step)
            for index, source in enumerate(sources):
                pltpu.make_async_remote_copy(
                    source.at[:, columns(other, head)],
                    target.at[head, index, rows],
                    send.at[head],
                    recv.at[head, y],
                    device_id=device,
                ).start()

    give(0, 0)

    @pl.when(has_next)
    def _():
        for head in range(LOCAL_HEADS):
            for index, source in enumerate((k_hbm, v_hbm)):
                pltpu.make_async_remote_copy(
                    source.at[:, columns(y, head)],
                    kv.at[head, index, own_rows],
                    halo_send.at[head],
                    halo_recv.at[head, y],
                    device_id=nxt,
                ).start()

    for step in range(1, GROUP):
        pltpu.make_async_remote_copy(
            fields_ref, field_rows.at[GROUP + y], field_send, field_recv, device_id=peer(step)[1]
        ).start()
    give(0, 1)
    give(1, 0)

    for step in range(1, copies):
        pl.semaphore_signal(rows_ready, inc=1, device_id=twin(step))

    def tell(turn):
        def act(other):
            pl.semaphore_signal(known.at[turn], inc=1, device_id={"seq": other})

        at_distance(2**turn, act)

    def hear(turn):
        pl.semaphore_wait(known.at[turn], count_at(2**turn))

    turns = (planes - 1).bit_length()
    tell(0)

    @pl.when(jnp.logical_not(has_prev))
    def _():
        kv[:, :, 0:WINDOW, :] = jnp.zeros((LOCAL_HEADS, 2, WINDOW, HEAD_DIM), kv.dtype)
        field_rows[0:GROUP] = jnp.full((GROUP, 1, TOK), -1, jnp.int32)

    plane_fields = field_rows.at[pl.ds(GROUP, GROUP)]
    halo_fields = field_rows.at[pl.ds(0, GROUP)]
    pltpu.make_async_copy(plane_fields, plane_fields, field_recv).wait()

    @pl.when(has_next)
    def _():
        pltpu.make_async_remote_copy(
            plane_fields, halo_fields, field_relay, field_halo, device_id=nxt
        ).start()

    def block_rows(first, source):
        return pl.ds(pl.multiple_of(first + source * TOK, TOK), TOK)

    def relay(head):
        own = kv.at[head, :, own_keys]
        pltpu.make_async_copy(own, own, kv_recv.at[head, y]).wait()
        for step in range(1, GROUP):
            source = lax.rem(y + GROUP - step, GROUP)
            arrived = kv.at[head, :, block_rows(WINDOW, source)]
            pltpu.make_async_copy(arrived, arrived, kv_recv.at[head, source]).wait()

            @pl.when(has_next)
            def _():
                pltpu.make_async_remote_copy(
                    arrived,
                    kv.at[head, :, block_rows(0, source)],
                    halo_send.at[head],
                    halo_recv.at[head, source],
                    device_id=nxt,
                ).start()

    relay(0)
    give(0, 2)

    @pl.when(has_prev)
    def _():
        pltpu.make_async_copy(halo_fields, halo_fields, field_halo).wait()

    lane = lax.broadcasted_iota(jnp.int32, (TOK, TOK), 1)
    row = lax.broadcasted_iota(jnp.int32, (TOK, TOK), 0)
    for part in range(2 * GROUP):
        by_lane = jnp.broadcast_to(field_rows[part].astype(jnp.float32), (TOK, TOK))
        by_row = by_lane.T
        by_field = by_lane == lax.rem(row, FIELDS).astype(jnp.float32)
        field_of_key[:, part * TOK : (part + 1) * TOK] = by_field.astype(jnp.float32).astype(jnp.bfloat16)
        chosen = by_row == lax.rem(lane, FIELDS).astype(jnp.float32)
        onehot[part * TOK : (part + 1) * TOK] = chosen.astype(jnp.float32).astype(jnp.bfloat16)

    field = lax.broadcasted_iota(jnp.int32, (FIELDS, 2 * FIELDS), 0)
    place = lax.broadcasted_iota(jnp.int32, (FIELDS, 2 * FIELDS), 1)
    twice = (lax.rem(place, FIELDS) == field).astype(jnp.float32).astype(jnp.bfloat16)
    scaled = dot(bias_ref[...], twice, NN) / SCALE
    high_part = scaled.astype(jnp.bfloat16).astype(jnp.float32)
    is_high = lax.broadcasted_iota(jnp.int32, (HEADS, 2 * FIELDS), 1) < FIELDS
    bias_rows[...] = jnp.where(is_high, high_part, scaled - high_part)

    older = row > lane
    older_low = older.astype(jnp.float32).astype(jnp.bfloat16)
    newer_low = 1.0 - older_low
    length = length_ref[0]
    unseen = jnp.where(has_prev, 0.0, MASKED)

    def work(head):
        for source in range(GROUP):
            here = qg.at[head, :, pl.ds(source * TOK, TOK)]
            pltpu.make_async_copy(here, here, qg_recv.at[head, source]).wait()

        @pl.when(has_prev)
        def _():
            for source in range(GROUP):
                halo = kv.at[head, :, pl.ds(source * TOK, TOK)]
                pltpu.make_async_copy(halo, halo, halo_recv.at[head, source]).wait()

        bias_row = bias_rows[pl.ds(y * LOCAL_HEADS + head, 1), :]
        bias_block = jnp.broadcast_to(bias_row, (TOK, TOK)).astype(jnp.bfloat16)
        for part in range(GROUP):
            first = part * TOK
            span = WINDOW + TOK
            seen = pl.ds(first, span)
            queries = qg[head, 0, first : first + TOK, :]
            grads = qg[head, 1, first : first + TOK, :]
            keys = kv[head, 0, seen, :]
            values = kv[head, 1, seen, :]
            logits = dot(
                jnp.concatenate([keys, onehot[seen, :]], axis=1),
                jnp.concatenate([queries, bias_block], axis=1),
                NT,
            )
            probs_grad = dot(values, grads, NT)

            def tiles(full):
                merged = jnp.where(older, full[0:TOK], full[WINDOW:span])
                return [merged] + [full[t * TOK : (t + 1) * TOK] for t in range(1, GROUP)]

            logit_tiles = tiles(logits)
            halo_tiles = GROUP - part
            logit_tiles = [
                (jnp.where(older, tile + unseen, tile) if t == 0 else tile + unseen)
                if t < halo_tiles
                else tile
                for t, tile in enumerate(logit_tiles)
            ]
            logit = jnp.concatenate(logit_tiles, axis=0)
            peak = jnp.max(logit, axis=0, keepdims=True)
            power = jnp.exp2((logit - peak) * (SCALE * LOG2E))
            total = jnp.sum(power, axis=0, keepdims=True)
            place = z * WINDOW + first + lax.broadcasted_iota(jnp.int32, (1, TOK), 1)
            share = jnp.where(place < length, 1.0 / total, 0.0)
            weight = power * share
            weight_low = weight.astype(jnp.bfloat16)
            prob = jnp.concatenate(tiles(probs_grad), axis=0)
            delta = jnp.sum(weight_low.astype(jnp.float32) * prob, axis=0, keepdims=True)
            grad = weight * (prob - delta)

            def spread(merged):
                top = merged[0:TOK]
                none = jnp.zeros_like(top)
                return jnp.concatenate(
                    [jnp.where(older, top, none), merged[TOK:WINDOW], jnp.where(older, none, top)],
                    axis=0,
                )

            def low_spread(merged):
                top = merged[0:TOK]
                return jnp.concatenate([top * older_low, merged[TOK:WINDOW], top * newer_low], axis=0)

            grad_full = spread(grad)
            grad_low = low_spread(grad.astype(jnp.bfloat16))
            weight_full = low_spread(weight_low)
            query_grad = dot(grad_low, keys, TN) * SCALE
            out_buf[head, 0, first : first + TOK, :] = query_grad.astype(jnp.bfloat16)
            key_part = dot(grad_low, queries, NN)
            value_part = dot(weight_full, grads, NN)
            for store, fresh in ((key_acc.at[0], key_part), (key_acc.at[1], value_part), (col_acc, grad_full)):
                if part == 0:
                    store[0:span, :] = fresh
                else:
                    store[first : first + WINDOW, :] += fresh[0:WINDOW]
                    store[first + WINDOW : first + span, :] = fresh[WINDOW:span]


        sums = col_acc[...]
        high = sums.astype(jnp.bfloat16)
        low = (sums - high.astype(jnp.float32)).astype(jnp.bfloat16)
        by_query = dot(field_of_key[...], high, NN) + dot(field_of_key[...], low, NN)
        bias_part[head] = jnp.sum(by_query.T, axis=0, keepdims=True)

    def give_back(head):
        ret_src[head, 0] = (key_acc[0, 0:WINDOW] * SCALE).astype(jnp.bfloat16)
        ret_src[head, 1] = key_acc[1, 0:WINDOW].astype(jnp.bfloat16)

        own_acc[head, 0] = key_acc[0, WINDOW:] * SCALE
        own_acc[head, 1] = key_acc[1, WINDOW:]

    def send_back(head):
        @pl.when(has_prev)
        def _():
            pltpu.make_async_remote_copy(
                ret_src.at[head],
                ret_dst.at[head],
                ret_send.at[head],
                ret_recv.at[head],
                device_id=prv,
            ).start()

    def give_query(head):
        for step in range(1, GROUP):
            other, device = peer(step)
            pltpu.make_async_remote_copy(
                out_buf.at[head, 0, pl.ds(pl.multiple_of(other * TOK, TOK), TOK)],
                dq_ref.at[:, columns(y, head)],
                outq_send.at[head],
                out_recv.at[0],
                device_id=device,
            ).start()
        pltpu.make_async_copy(
            out_buf.at[head, 0, own_rows], dq_ref.at[:, columns(y, head)], out_recv.at[0]
        ).start()

    def finish(head):
        @pl.when(has_next)
        def _():
            back = ret_dst.at[head]
            pltpu.make_async_copy(back, back, ret_recv.at[head]).wait()
            for index in range(2):
                out_buf[head, 1 + index] = (
                    own_acc[head, index] + ret_dst[head, index].astype(jnp.float32)
                ).astype(jnp.bfloat16)

        @pl.when(jnp.logical_not(has_next))
        def _():
            for index in range(2):
                out_buf[head, 1 + index] = own_acc[head, index].astype(jnp.bfloat16)

        for index, result in ((1, dk_ref), (2, dv_ref)):
            for step in range(1, GROUP):
                other, device = peer(step)
                pltpu.make_async_remote_copy(
                    out_buf.at[head, index, pl.ds(pl.multiple_of(other * TOK, TOK), TOK)],
                    result.at[:, columns(y, head)],
                    outkv_send.at[head],
                    out_recv.at[index],
                    device_id=device,
                ).start()
            pltpu.make_async_copy(
                out_buf.at[head, index, own_rows], result.at[:, columns(y, head)], out_recv.at[index]
            ).start()

    hear(0)
    tell(1)
    relay(1)
    give(0, 3)
    give(1, 1)

    @pl.loop(0, LOCAL_HEADS)
    def _(head):
        for turn in range(1, turns - 1):

            @pl.when(head == min(turn - 1, LOCAL_HEADS - 1))
            def _():
                hear(turn)
                tell(turn + 1)

        @pl.when(head == LOCAL_HEADS - 2)
        def _():
            for ready in range(LOCAL_HEADS - 2):
                give_query(ready)

        work(head)

        @pl.when(head == 0)
        def _():
            for later in range(2, LOCAL_HEADS):
                relay(later)
                give(1, later)

        @pl.when(head == LOCAL_HEADS - 1)
        def _():
            for pair in range(LOCAL_HEADS // 2):
                mine[pair] = jnp.where(is_high[0:1], bias_part[2 * pair], bias_part[2 * pair + 1])
            plane_parts[z] = mine[...]
            hear(turns - 1)

            @pl.loop(0, planes - 1)
            def _(step):
                target = step + (step >= z).astype(jnp.int32)
                pltpu.make_async_remote_copy(
                    mine,
                    plane_parts.at[z],
                    plane_send,
                    plane_recv,
                    device_id={"seq": target * GROUP + y},
                ).start()

        give_back(head)

        @pl.when(head < LOCAL_HEADS - 2)
        def _():
            send_back(head)


    def rest_of(parts):
        return parts.at[pl.ds(0, parts.shape[0] - 1)]

    def landed(parts, sem):
        pltpu.make_async_copy(rest_of(parts), rest_of(parts), sem).wait()

    def sum_of(parts):
        total = parts[0]
        for index in range(1, parts.shape[0]):
            total = total + parts[index]
        return total

    send_back(LOCAL_HEADS - 2)
    send_back(LOCAL_HEADS - 1)
    give_query(LOCAL_HEADS - 2)
    give_query(LOCAL_HEADS - 1)
    for head in range(LOCAL_HEADS):
        finish(head)

    landed(plane_parts, plane_recv)
    mate_parts[seat] = sum_of(plane_parts)
    pl.semaphore_wait(rows_ready, copies - 1)

    @pl.loop(0, mates - 1)
    def _(turn):
        step = 1 + lax.rem(turn + 2 * GROUP, mates - 1)
        other = lax.rem(seat + step, mates)
        part = mate_parts.at[seat]
        pltpu.make_async_remote_copy(
            part,
            part,
            mate_send,
            mate_recv,
            device_id={"seq": z * GROUP + lax.rem(other, GROUP), "dp": other // GROUP},
        ).start()

    for parts, sem in ((plane_parts, plane_send), (mate_parts, mate_send)):
        landed(parts, sem)
    sent_fields = field_rows.at[pl.ds(0, GROUP - 1)]
    pltpu.make_async_copy(sent_fields, sent_fields, field_send).wait()

    @pl.when(has_next)
    def _():
        pltpu.make_async_copy(halo_fields, halo_fields, field_relay).wait()

    @pl.loop(0, LOCAL_HEADS)
    def _(head):
        sent = kv.at[head, :, pl.ds(0, WINDOW - TOK)]
        pltpu.make_async_copy(sent, sent, kv_send.at[head]).wait()
        pltpu.make_async_copy(sent, sent, qg_send.at[head]).wait()
        pltpu.make_async_copy(sent, sent, outkv_send.at[head]).wait()
        query_sent = kv.at[head, 0, pl.ds(0, WINDOW - TOK)]
        pltpu.make_async_copy(query_sent, query_sent, outq_send.at[head]).wait()

        @pl.when(has_next)
        def _():
            halo = kv.at[head, :, pl.ds(0, WINDOW)]
            pltpu.make_async_copy(halo, halo, halo_send.at[head]).wait()

        @pl.when(has_prev)
        def _():
            source = ret_src.at[head]
            pltpu.make_async_copy(source, source, ret_send.at[head]).wait()

    for index, result in enumerate((dq_ref, dk_ref, dv_ref)):
        pltpu.make_async_copy(result, result, out_recv.at[index]).wait()

    landed(mate_parts, mate_recv)
    for owner in range(GROUP):
        for pair in range(LOCAL_HEADS // 2):
            both = mate_parts[owner, pair]
            for copy in range(1, copies):
                both = both + mate_parts[copy * GROUP + owner, pair]
            first = owner * LOCAL_HEADS + 2 * pair
            dbias_ref[first : first + 1, :] = both[:, 0:FIELDS]
            dbias_ref[first + 1 : first + 2, :] = pltpu.roll(both, FIELDS, 1)[:, 0:FIELDS]


def copy_kernel(*refs):
    count = len(refs) // 2
    sources, targets, sems = refs[:count], refs[count : 2 * count], refs[-1]
    moves = [
        pltpu.make_async_copy(sources[index], targets[index], sems.at[index]) for index in range(count)
    ]
    for move in moves:
        move.start()
    for move in moves:
        move.wait()


def shards(planes, copies, queries, keys, values, grad_out, lengths, fields, field_bias):
    tok_rows, row_width = queries.shape[1:]
    low_type, full_type = jnp.bfloat16, jnp.float32
    grads_shape = jax.ShapeDtypeStruct((tok_rows, row_width), low_type)
    in_hbm = pl.BlockSpec(memory_space=pltpu.HBM)
    in_vmem = pl.BlockSpec(memory_space=pltpu.VMEM)
    dma = pltpu.SemaphoreType.DMA
    heads = LOCAL_HEADS
    query_grad, key_grad, value_grad, bias_total = pl.pallas_call(
        functools.partial(kernel, planes, copies),
        out_shape=(
            pltpu.VMEM(grads_shape.shape, low_type),
            pltpu.VMEM(grads_shape.shape, low_type),
            pltpu.VMEM(grads_shape.shape, low_type),
            pltpu.VMEM((HEADS, FIELDS), full_type),
        ),
        in_specs=[
            pl.BlockSpec(memory_space=pltpu.SMEM),
            in_vmem,
            in_vmem,
            in_hbm,
            in_hbm,
            in_hbm,
            in_hbm,
        ],
        out_specs=(in_vmem, in_vmem, in_vmem, in_vmem),
        scratch_shapes=[
            pltpu.VMEM((HEADS, 2 * FIELDS), full_type),
            pltpu.VMEM((heads, 1, 2 * FIELDS), full_type),
            pltpu.VMEM((heads // 2, 1, 2 * FIELDS), full_type),
            pltpu.VMEM((planes, heads // 2, 1, 2 * FIELDS), full_type),
            pltpu.VMEM((copies * GROUP, heads // 2, 1, 2 * FIELDS), full_type),
            pltpu.VMEM((heads, 2, 2 * WINDOW, HEAD_DIM), low_type),
            pltpu.VMEM((heads, 2, WINDOW, HEAD_DIM), low_type),
            pltpu.VMEM((2 * GROUP, 1, TOK), jnp.int32),
            pltpu.VMEM((2 * WINDOW, 2 * FIELDS), low_type),
            pltpu.VMEM((2 * FIELDS, 2 * WINDOW), low_type),
            pltpu.VMEM((2, 2 * WINDOW, HEAD_DIM), full_type),
            pltpu.VMEM((heads, 2, WINDOW, HEAD_DIM), full_type),
            pltpu.VMEM((2 * WINDOW, HEAD_DIM), full_type),
            pltpu.VMEM((heads, 2, WINDOW, HEAD_DIM), low_type),
            pltpu.VMEM((heads, 2, WINDOW, HEAD_DIM), low_type),
            pltpu.VMEM((heads, 3, WINDOW, HEAD_DIM), low_type),
            dma,
            dma,
            dma,
            dma,
            dma((heads,)),
            dma((heads, GROUP)),
            dma((heads,)),
            dma((heads, GROUP)),
            dma((heads,)),
            dma((heads, GROUP)),
            dma((heads,)),
            dma((heads,)),
            dma((heads,)),
            dma((heads,)),
            dma((3,)),
            dma,
            dma,
            dma,
            dma,
            pltpu.SemaphoreType.REGULAR,
            pltpu.SemaphoreType.REGULAR(((planes - 1).bit_length(),)),
        ],
        compiler_params=pltpu.CompilerParams(
            collective_id=0, has_side_effects=True, vmem_limit_bytes=60 * 2**20
        ),
    )(lengths, field_bias, fields, queries[0], keys[0], values[0], grad_out[0])
    results = (query_grad, key_grad, value_grad, bias_total)
    query_grad, key_grad, value_grad, bias_total = pl.pallas_call(
        copy_kernel,
        out_shape=tuple(jax.ShapeDtypeStruct(one.shape, one.dtype) for one in results),
        in_specs=[in_vmem] * 4,
        out_specs=(in_hbm,) * 4,
        scratch_shapes=[dma((4,))],
        compiler_params=pltpu.CompilerParams(vmem_limit_bytes=2**20),
    )(*results)
    return query_grad[None], key_grad[None], value_grad[None], bias_total


def solution(mesh):
    rows = P("dp", "seq", None)
    return jax.shard_map(
        functools.partial(shards, mesh.shape["seq"] // GROUP, mesh.shape["dp"]),
        mesh=mesh,
        in_specs=(rows, rows, rows, rows, P("dp"), P("dp", "seq"), P()),
        out_specs=(rows, rows, rows, P()),
        check_vma=False,
    )
```

```python
import functools

import jax
import jax.numpy as jnp
from jax import lax
from jax.experimental import pallas as pl
from jax.experimental.pallas import tpu as pltpu
from jax.sharding import PartitionSpec as P

HEADS = 16
HEAD_DIM = 128
WINDOW = 512
FIELDS = 64
TOK = 128
GROUP = WINDOW // TOK
LOCAL_HEADS = HEADS // GROUP
PIECES = 4
SCALE = HEAD_DIM**-0.5
LOG2E = 1.4426950408889634
MASKED = -1e30
NT = (((1,), (1,)), ((), ()))
NN = (((1,), (0,)), ((), ()))
TN = (((0,), (0,)), ((), ()))


def dot(lhs, rhs, dims):
    return lax.dot_general(lhs, rhs, dims, preferred_element_type=jnp.float32)


def kernel(
    planes,
    copies,
    length_ref,
    bias_ref,
    fields_ref,
    q_hbm,
    k_hbm,
    v_hbm,
    g_hbm,
    dq_ref,
    dk_ref,
    dv_ref,
    dbias_ref,
    bias_rows,
    bias_part,
    mine,
    plane_parts,
    mate_parts,
    kv,
    qg,
    field_rows,
    onehot,
    field_of_key,
    key_acc,
    own_acc,
    col_acc,
    ret_src,
    ret_dst,
    out_buf,
    field_send,
    field_recv,
    field_relay,
    field_halo,
    kv_send,
    kv_recv,
    qg_send,
    qg_recv,
    halo_send,
    halo_recv,
    ret_send,
    ret_recv,
    outq_send,
    outkv_send,
    out_recv,
    plane_send,
    plane_recv,
    mate_send,
    mate_recv,
    rows_ready,
    known,
):
    block = lax.axis_index("seq")
    sequence = lax.axis_index("dp")
    y = lax.rem(block, GROUP)
    z = block // GROUP
    has_prev = z > 0
    has_next = z < planes - 1

    def peer(step):
        other = lax.rem(y + step, GROUP)
        return other, {"seq": z * GROUP + other}

    nxt = {"seq": block + GROUP}
    prv = {"seq": block - GROUP}

    mates = copies * GROUP
    seat = sequence * GROUP + y

    def at_distance(distance, act):
        @pl.when(z >= distance)
        def _():
            act(block - distance * GROUP)

        @pl.when(z + distance < planes)
        def _():
            act(block + distance * GROUP)

    def count_at(distance):
        below = (z >= distance).astype(jnp.int32)
        return below + (z + distance < planes).astype(jnp.int32)

    barrier = pltpu.get_barrier_semaphore()

    def greet(other):
        pl.semaphore_signal(barrier, inc=1, device_id={"seq": other})

    def twin(step):
        return {"dp": lax.rem(sequence + step, copies)}

    for step in range(1, GROUP):
        pl.semaphore_signal(barrier, inc=1, device_id=peer(step)[1])
    at_distance(1, greet)
    for step in range(1, copies):
        pl.semaphore_signal(barrier, inc=1, device_id=twin(step))
    own_rows = pl.ds(pl.multiple_of(y * TOK, TOK), TOK)
    own_keys = pl.ds(pl.multiple_of(WINDOW + y * TOK, TOK), TOK)
    plane_keys = pl.ds(WINDOW, WINDOW)

    def columns(owner, head):
        return pl.ds(pl.multiple_of((owner * LOCAL_HEADS + head) * HEAD_DIM, HEAD_DIM), HEAD_DIM)

    arrays = ((kv_send, kv_recv, (k_hbm, v_hbm), kv, own_keys), (qg_send, qg_recv, (q_hbm, g_hbm), qg, own_rows))

    pltpu.make_async_copy(fields_ref, field_rows.at[GROUP + y], field_recv).start()
    for head in range(LOCAL_HEADS):
        for _, recv, sources, target, rows in arrays:
            for index, source in enumerate(sources):
                pltpu.make_async_copy(
                    source.at[:, columns(y, head)], target.at[head, index, rows], recv.at[head, y]
                ).start()

    pl.semaphore_wait(barrier, GROUP + copies - 2 + count_at(1))

    def give(kind, head):
        send, recv, sources, target, rows = arrays[kind]
        for step in range(1, GROUP):
            other, device = peer(step)
            for index, source in enumerate(sources):
                pltpu.make_async_remote_copy(
                    source.at[:, columns(other, head)],
                    target.at[head, index, rows],
                    send.at[head],
                    recv.at[head, y],
                    device_id=device,
                ).start()

    give(0, 0)

    @pl.when(has_next)
    def _():
        for head in range(LOCAL_HEADS):
            for index, source in enumerate((k_hbm, v_hbm)):
                pltpu.make_async_remote_copy(
                    source.at[:, columns(y, head)],
                    kv.at[head, index, own_rows],
                    halo_send.at[head],
                    halo_recv.at[head, y],
                    device_id=nxt,
                ).start()

    for step in range(1, GROUP):
        pltpu.make_async_remote_copy(
            fields_ref, field_rows.at[GROUP + y], field_send, field_recv, device_id=peer(step)[1]
        ).start()
    give(0, 1)
    give(1, 0)

    for step in range(1, copies):
        pl.semaphore_signal(rows_ready, inc=1, device_id=twin(step))

    def tell(turn):
        def act(other):
            pl.semaphore_signal(known.at[turn], inc=1, device_id={"seq": other})

        at_distance(2**turn, act)

    def hear(turn):
        pl.semaphore_wait(known.at[turn], count_at(2**turn))

    turns = (planes - 1).bit_length()
    tell(0)

    @pl.when(jnp.logical_not(has_prev))
    def _():
        kv[:, :, 0:WINDOW, :] = jnp.zeros((LOCAL_HEADS, 2, WINDOW, HEAD_DIM), kv.dtype)
        field_rows[0:GROUP] = jnp.full((GROUP, 1, TOK), -1, jnp.int32)

    plane_fields = field_rows.at[pl.ds(GROUP, GROUP)]
    halo_fields = field_rows.at[pl.ds(0, GROUP)]
    pltpu.make_async_copy(plane_fields, plane_fields, field_recv).wait()

    @pl.when(has_next)
    def _():
        pltpu.make_async_remote_copy(
            plane_fields, halo_fields, field_relay, field_halo, device_id=nxt
        ).start()

    def block_rows(first, source):
        return pl.ds(pl.multiple_of(first + source * TOK, TOK), TOK)

    def relay(head):
        own = kv.at[head, :, own_keys]
        pltpu.make_async_copy(own, own, kv_recv.at[head, y]).wait()
        for step in range(1, GROUP):
            source = lax.rem(y + GROUP - step, GROUP)
            arrived = kv.at[head, :, block_rows(WINDOW, source)]
            pltpu.make_async_copy(arrived, arrived, kv_recv.at[head, source]).wait()

            @pl.when(has_next)
            def _():
                pltpu.make_async_remote_copy(
                    arrived,
                    kv.at[head, :, block_rows(0, source)],
                    halo_send.at[head],
                    halo_recv.at[head, source],
                    device_id=nxt,
                ).start()

    relay(0)
    give(0, 2)

    @pl.when(has_prev)
    def _():
        pltpu.make_async_copy(halo_fields, halo_fields, field_halo).wait()

    lane = lax.broadcasted_iota(jnp.int32, (TOK, TOK), 1)
    row = lax.broadcasted_iota(jnp.int32, (TOK, TOK), 0)
    for part in range(2 * GROUP):
        by_lane = jnp.broadcast_to(field_rows[part].astype(jnp.float32), (TOK, TOK))
        by_row = by_lane.T
        by_field = by_lane == lax.rem(row, FIELDS).astype(jnp.float32)
        field_of_key[:, part * TOK : (part + 1) * TOK] = by_field.astype(jnp.float32).astype(jnp.bfloat16)
        chosen = by_row == lax.rem(lane, FIELDS).astype(jnp.float32)
        onehot[part * TOK : (part + 1) * TOK] = chosen.astype(jnp.float32).astype(jnp.bfloat16)

    field = lax.broadcasted_iota(jnp.int32, (FIELDS, 2 * FIELDS), 0)
    place = lax.broadcasted_iota(jnp.int32, (FIELDS, 2 * FIELDS), 1)
    twice = (lax.rem(place, FIELDS) == field).astype(jnp.float32).astype(jnp.bfloat16)
    scaled = dot(bias_ref[...], twice, NN) / SCALE
    high_part = scaled.astype(jnp.bfloat16).astype(jnp.float32)
    is_high = lax.broadcasted_iota(jnp.int32, (HEADS, 2 * FIELDS), 1) < FIELDS
    bias_rows[...] = jnp.where(is_high, high_part, scaled - high_part)

    older = row > lane
    older_low = older.astype(jnp.float32).astype(jnp.bfloat16)
    newer_low = 1.0 - older_low
    length = length_ref[0]
    unseen = jnp.where(has_prev, 0.0, MASKED)

    def work(head):
        for source in range(GROUP):
            here = qg.at[head, :, pl.ds(source * TOK, TOK)]
            pltpu.make_async_copy(here, here, qg_recv.at[head, source]).wait()

        @pl.when(has_prev)
        def _():
            for source in range(GROUP):
                halo = kv.at[head, :, pl.ds(source * TOK, TOK)]
                pltpu.make_async_copy(halo, halo, halo_recv.at[head, source]).wait()

        bias_row = bias_rows[pl.ds(y * LOCAL_HEADS + head, 1), :]
        bias_block = jnp.broadcast_to(bias_row, (TOK, TOK)).astype(jnp.bfloat16)
        for part in range(GROUP):
            first = part * TOK
            span = WINDOW + TOK
            seen = pl.ds(first, span)
            queries = qg[head, 0, first : first + TOK, :]
            grads = qg[head, 1, first : first + TOK, :]
            keys = kv[head, 0, seen, :]
            values = kv[head, 1, seen, :]
            logits = dot(
                jnp.concatenate([keys, onehot[seen, :]], axis=1),
                jnp.concatenate([queries, bias_block], axis=1),
                NT,
            )
            probs_grad = dot(values, grads, NT)

            def tiles(full):
                merged = jnp.where(older, full[0:TOK], full[WINDOW:span])
                return [merged] + [full[t * TOK : (t + 1) * TOK] for t in range(1, GROUP)]

            logit_tiles = tiles(logits)
            halo_tiles = GROUP - part
            logit_tiles = [
                (jnp.where(older, tile + unseen, tile) if t == 0 else tile + unseen)
                if t < halo_tiles
                else tile
                for t, tile in enumerate(logit_tiles)
            ]
            logit = jnp.concatenate(logit_tiles, axis=0)
            peak = jnp.max(logit, axis=0, keepdims=True)
            power = jnp.exp2((logit - peak) * (SCALE * LOG2E))
            total = jnp.sum(power, axis=0, keepdims=True)
            place = z * WINDOW + first + lax.broadcasted_iota(jnp.int32, (1, TOK), 1)
            share = jnp.where(place < length, 1.0 / total, 0.0)
            weight = power * share
            weight_low = weight.astype(jnp.bfloat16)
            prob = jnp.concatenate(tiles(probs_grad), axis=0)
            delta = jnp.sum(weight_low.astype(jnp.float32) * prob, axis=0, keepdims=True)
            grad = weight * (prob - delta)

            def spread(merged):
                top = merged[0:TOK]
                none = jnp.zeros_like(top)
                return jnp.concatenate(
                    [jnp.where(older, top, none), merged[TOK:WINDOW], jnp.where(older, none, top)],
                    axis=0,
                )

            def low_spread(merged):
                top = merged[0:TOK]
                return jnp.concatenate([top * older_low, merged[TOK:WINDOW], top * newer_low], axis=0)

            grad_full = spread(grad)
            grad_low = low_spread(grad.astype(jnp.bfloat16))
            weight_full = low_spread(weight_low)
            query_grad = dot(grad_low, keys, TN) * SCALE
            out_buf[head, 0, first : first + TOK, :] = query_grad.astype(jnp.bfloat16)
            key_part = dot(grad_low, queries, NN)
            value_part = dot(weight_full, grads, NN)
            for store, fresh in ((key_acc.at[0], key_part), (key_acc.at[1], value_part), (col_acc, grad_full)):
                if part == 0:
                    store[0:span, :] = fresh
                else:
                    store[first : first + WINDOW, :] += fresh[0:WINDOW]
                    store[first + WINDOW : first + span, :] = fresh[WINDOW:span]


        sums = col_acc[...]
        high = sums.astype(jnp.bfloat16)
        low = (sums - high.astype(jnp.float32)).astype(jnp.bfloat16)
        by_query = dot(field_of_key[...], high, NN) + dot(field_of_key[...], low, NN)
        bias_part[head] = jnp.sum(by_query.T, axis=0, keepdims=True)

    def give_back(head):
        ret_src[head, 0] = (key_acc[0, 0:WINDOW] * SCALE).astype(jnp.bfloat16)
        ret_src[head, 1] = key_acc[1, 0:WINDOW].astype(jnp.bfloat16)

        own_acc[head, 0] = key_acc[0, WINDOW:] * SCALE
        own_acc[head, 1] = key_acc[1, WINDOW:]

    def send_back(head):
        @pl.when(has_prev)
        def _():
            pltpu.make_async_remote_copy(
                ret_src.at[head],
                ret_dst.at[head],
                ret_send.at[head],
                ret_recv.at[head],
                device_id=prv,
            ).start()

    def give_query(head):
        for step in range(1, GROUP):
            other, device = peer(step)
            pltpu.make_async_remote_copy(
                out_buf.at[head, 0, pl.ds(pl.multiple_of(other * TOK, TOK), TOK)],
                dq_ref.at[:, columns(y, head)],
                outq_send.at[head],
                out_recv.at[0],
                device_id=device,
            ).start()
        pltpu.make_async_copy(
            out_buf.at[head, 0, own_rows], dq_ref.at[:, columns(y, head)], out_recv.at[0]
        ).start()

    def finish(head):
        @pl.when(has_next)
        def _():
            back = ret_dst.at[head]
            pltpu.make_async_copy(back, back, ret_recv.at[head]).wait()
            for index in range(2):
                out_buf[head, 1 + index] = (
                    own_acc[head, index] + ret_dst[head, index].astype(jnp.float32)
                ).astype(jnp.bfloat16)

        @pl.when(jnp.logical_not(has_next))
        def _():
            for index in range(2):
                out_buf[head, 1 + index] = own_acc[head, index].astype(jnp.bfloat16)

        for index, result in ((1, dk_ref), (2, dv_ref)):
            for step in range(1, GROUP):
                other, device = peer(step)
                pltpu.make_async_remote_copy(
                    out_buf.at[head, index, pl.ds(pl.multiple_of(other * TOK, TOK), TOK)],
                    result.at[:, columns(y, head)],
                    outkv_send.at[head],
                    out_recv.at[index],
                    device_id=device,
                ).start()
            pltpu.make_async_copy(
                out_buf.at[head, index, own_rows], result.at[:, columns(y, head)], out_recv.at[index]
            ).start()

    hear(0)
    tell(1)
    relay(1)
    give(0, 3)
    give(1, 1)

    @pl.loop(0, LOCAL_HEADS)
    def _(head):
        for turn in range(1, turns - 1):

            @pl.when(head == min(turn - 1, LOCAL_HEADS - 1))
            def _():
                hear(turn)
                tell(turn + 1)

        @pl.when(head == LOCAL_HEADS - 2)
        def _():
            for ready in range(LOCAL_HEADS - 2):
                give_query(ready)

        work(head)

        @pl.when(head == 0)
        def _():
            for later in range(2, LOCAL_HEADS):
                relay(later)
                give(1, later)

        @pl.when(head == LOCAL_HEADS - 1)
        def _():
            for pair in range(LOCAL_HEADS // 2):
                mine[pair] = jnp.where(is_high[0:1], bias_part[2 * pair], bias_part[2 * pair + 1])
            plane_parts[z] = mine[...]
            hear(turns - 1)

            @pl.loop(0, planes - 1)
            def _(step):
                target = step + (step >= z).astype(jnp.int32)
                pltpu.make_async_remote_copy(
                    mine,
                    plane_parts.at[z],
                    plane_send,
                    plane_recv,
                    device_id={"seq": target * GROUP + y},
                ).start()

        give_back(head)

        @pl.when(head < LOCAL_HEADS - 2)
        def _():
            send_back(head)


    def rest_of(parts):
        return parts.at[pl.ds(0, parts.shape[0] - 1)]

    def landed(parts, sem):
        pltpu.make_async_copy(rest_of(parts), rest_of(parts), sem).wait()

    def sum_of(parts):
        total = parts[0]
        for index in range(1, parts.shape[0]):
            total = total + parts[index]
        return total

    send_back(LOCAL_HEADS - 2)
    send_back(LOCAL_HEADS - 1)
    give_query(LOCAL_HEADS - 2)
    give_query(LOCAL_HEADS - 1)
    for head in range(LOCAL_HEADS):
        finish(head)

    landed(plane_parts, plane_recv)
    mate_parts[seat] = sum_of(plane_parts)
    pl.semaphore_wait(rows_ready, copies - 1)

    @pl.loop(0, mates - 1)
    def _(turn):
        step = 1 + lax.rem(turn + 2 * GROUP, mates - 1)
        other = lax.rem(seat + step, mates)
        part = mate_parts.at[seat]
        pltpu.make_async_remote_copy(
            part,
            part,
            mate_send,
            mate_recv,
            device_id={"seq": z * GROUP + lax.rem(other, GROUP), "dp": other // GROUP},
        ).start()

    for parts, sem in ((plane_parts, plane_send), (mate_parts, mate_send)):
        landed(parts, sem)
    sent_fields = field_rows.at[pl.ds(0, GROUP - 1)]
    pltpu.make_async_copy(sent_fields, sent_fields, field_send).wait()

    @pl.when(has_next)
    def _():
        pltpu.make_async_copy(halo_fields, halo_fields, field_relay).wait()

    @pl.loop(0, LOCAL_HEADS)
    def _(head):
        sent = kv.at[head, :, pl.ds(0, WINDOW - TOK)]
        pltpu.make_async_copy(sent, sent, kv_send.at[head]).wait()
        pltpu.make_async_copy(sent, sent, qg_send.at[head]).wait()
        pltpu.make_async_copy(sent, sent, outkv_send.at[head]).wait()
        query_sent = kv.at[head, 0, pl.ds(0, WINDOW - TOK)]
        pltpu.make_async_copy(query_sent, query_sent, outq_send.at[head]).wait()

        @pl.when(has_next)
        def _():
            halo = kv.at[head, :, pl.ds(0, WINDOW)]
            pltpu.make_async_copy(halo, halo, halo_send.at[head]).wait()

        @pl.when(has_prev)
        def _():
            source = ret_src.at[head]
            pltpu.make_async_copy(source, source, ret_send.at[head]).wait()

    for index, result in enumerate((dq_ref, dk_ref, dv_ref)):
        pltpu.make_async_copy(result, result, out_recv.at[index]).wait()

    landed(mate_parts, mate_recv)
    for owner in range(GROUP):
        for pair in range(LOCAL_HEADS // 2):
            both = mate_parts[owner, pair]
            for copy in range(1, copies):
                both = both + mate_parts[copy * GROUP + owner, pair]
            first = owner * LOCAL_HEADS + 2 * pair
            dbias_ref[first : first + 1, :] = both[:, 0:FIELDS]
            dbias_ref[first + 1 : first + 2, :] = pltpu.roll(both, FIELDS, 1)[:, 0:FIELDS]


def copy_kernel(*refs):
    count = len(refs) // 2
    sources, targets, sems = refs[:count], refs[count : 2 * count], refs[-1]
    moves = []
    for index in range(count):
        rows = sources[index].shape[0]
        piece = max(rows // PIECES, 16)
        for turn, first in enumerate(range(0, rows, piece)):
            part = pl.ds(first, piece)
            moves.append(
                pltpu.make_async_copy(
                    sources[index].at[part], targets[index].at[part], sems.at[index, turn]
                )
            )
    for move in moves:
        move.start()
    for move in moves:
        move.wait()


def shards(planes, copies, queries, keys, values, grad_out, lengths, fields, field_bias):
    tok_rows, row_width = queries.shape[1:]
    low_type, full_type = jnp.bfloat16, jnp.float32
    grads_shape = jax.ShapeDtypeStruct((tok_rows, row_width), low_type)
    in_hbm = pl.BlockSpec(memory_space=pltpu.HBM)
    in_vmem = pl.BlockSpec(memory_space=pltpu.VMEM)
    dma = pltpu.SemaphoreType.DMA
    heads = LOCAL_HEADS
    query_grad, key_grad, value_grad, bias_total = pl.pallas_call(
        functools.partial(kernel, planes, copies),
        out_shape=(
            pltpu.VMEM(grads_shape.shape, low_type),
            pltpu.VMEM(grads_shape.shape, low_type),
            pltpu.VMEM(grads_shape.shape, low_type),
            pltpu.VMEM((HEADS, FIELDS), full_type),
        ),
        in_specs=[
            pl.BlockSpec(memory_space=pltpu.SMEM),
            in_vmem,
            in_vmem,
            in_hbm,
            in_hbm,
            in_hbm,
            in_hbm,
        ],
        out_specs=(in_vmem, in_vmem, in_vmem, in_vmem),
        scratch_shapes=[
            pltpu.VMEM((HEADS, 2 * FIELDS), full_type),
            pltpu.VMEM((heads, 1, 2 * FIELDS), full_type),
            pltpu.VMEM((heads // 2, 1, 2 * FIELDS), full_type),
            pltpu.VMEM((planes, heads // 2, 1, 2 * FIELDS), full_type),
            pltpu.VMEM((copies * GROUP, heads // 2, 1, 2 * FIELDS), full_type),
            pltpu.VMEM((heads, 2, 2 * WINDOW, HEAD_DIM), low_type),
            pltpu.VMEM((heads, 2, WINDOW, HEAD_DIM), low_type),
            pltpu.VMEM((2 * GROUP, 1, TOK), jnp.int32),
            pltpu.VMEM((2 * WINDOW, 2 * FIELDS), low_type),
            pltpu.VMEM((2 * FIELDS, 2 * WINDOW), low_type),
            pltpu.VMEM((2, 2 * WINDOW, HEAD_DIM), full_type),
            pltpu.VMEM((heads, 2, WINDOW, HEAD_DIM), full_type),
            pltpu.VMEM((2 * WINDOW, HEAD_DIM), full_type),
            pltpu.VMEM((heads, 2, WINDOW, HEAD_DIM), low_type),
            pltpu.VMEM((heads, 2, WINDOW, HEAD_DIM), low_type),
            pltpu.VMEM((heads, 3, WINDOW, HEAD_DIM), low_type),
            dma,
            dma,
            dma,
            dma,
            dma((heads,)),
            dma((heads, GROUP)),
            dma((heads,)),
            dma((heads, GROUP)),
            dma((heads,)),
            dma((heads, GROUP)),
            dma((heads,)),
            dma((heads,)),
            dma((heads,)),
            dma((heads,)),
            dma((3,)),
            dma,
            dma,
            dma,
            dma,
            pltpu.SemaphoreType.REGULAR,
            pltpu.SemaphoreType.REGULAR(((planes - 1).bit_length(),)),
        ],
        compiler_params=pltpu.CompilerParams(
            collective_id=0, has_side_effects=True, vmem_limit_bytes=60 * 2**20
        ),
    )(lengths, field_bias, fields, queries[0], keys[0], values[0], grad_out[0])
    results = (query_grad, key_grad, value_grad, bias_total)
    query_grad, key_grad, value_grad, bias_total = pl.pallas_call(
        copy_kernel,
        out_shape=tuple(jax.ShapeDtypeStruct(one.shape, one.dtype) for one in results),
        in_specs=[in_vmem] * 4,
        out_specs=(in_hbm,) * 4,
        scratch_shapes=[dma((4, PIECES))],
        compiler_params=pltpu.CompilerParams(vmem_limit_bytes=2**20),
    )(*results)
    return query_grad[None], key_grad[None], value_grad[None], bias_total


def solution(mesh):
    rows = P("dp", "seq", None)
    return jax.shard_map(
        functools.partial(shards, mesh.shape["seq"] // GROUP, mesh.shape["dp"]),
        mesh=mesh,
        in_specs=(rows, rows, rows, rows, P("dp"), P("dp", "seq"), P()),
        out_specs=(rows, rows, rows, P()),
        check_vma=False,
    )
```
